32 devices in a mesh: dp: 2 (over core), row: 4 (over y, x), col: 4 (over z).
Axes of the slice: x: 2, y: 2, z: 4, core: 2. Of those that a mesh axis runs over, the one named last changes fastest.
Arguments:
- tokens: bfloat16 [4096, 2048], P(('dp', 'row'), 'col'), may hold values from -6 to 6
- mixer_norm: float32 [2048], P('col'), may hold values from 0.1 to 1.9
- in_value: float32 [2048, 4096], P('col', 'row'), may hold values from -0.125 to 0.125
- in_gate: float32 [2048, 4096], P('col', 'row'), may hold values from -0.125 to 0.125
- conv_weight: float32 [4096, 4], P(('row', 'col')), may hold values from -3 to 3
- conv_bias: float32 [4096], P(('row', 'col')), may hold values from -4 to 4
- state_proj: float32 [4096, 160], P(('row', 'col')), may hold values from -0.25 to 0.25
- step_proj: float32 [128, 4096], P(None, ('row', 'col')), may hold values from -0.5 to 0.5
- step_bias: float32 [4096], P(('row', 'col')), may hold values from -5 to -2
- decay_log: float32 [4096, 16], P(('row', 'col')), may hold values from 0 to 2.8
- skip_gain: float32 [4096], P(('row', 'col')), may hold values from 0.5 to 1.5
- mixer_out: float32 [4096, 2048], P('row', 'col'), may hold values from -0.1875 to 0.1875
- feed_norm: float32 [2048], P('col'), may hold values from 0.1 to 1.9
- feed_gate: float32 [2048, 8192], P('col', 'row'), may hold values from -0.125 to 0.125
- feed_up: float32 [2048, 8192], P('col', 'row'), may hold values from -0.125 to 0.125
- feed_down: float32 [8192, 2048], P('row', 'col'), may hold values from -0.09375 to 0.09375
- out_grad: bfloat16 [4096, 2048], P(('dp', 'row'), 'col'), may hold values from -6 to 6
Outputs:
- output: bfloat16 [4096, 2048], P(('dp', 'row'), 'col')
- tokens_grad: float32 [4096, 2048], P(('dp', 'row'), 'col')
- mixer_norm_grad: float32 [2048], P('col')
- in_value_grad: float32 [2048, 4096], P('col', 'row')
- in_gate_grad: float32 [2048, 4096], P('col', 'row')
- conv_weight_grad: float32 [4096, 4], P(('row', 'col'))
- conv_bias_grad: float32 [4096], P(('row', 'col'))
- state_proj_grad: float32 [4096, 160], P(('row', 'col'))
- step_proj_grad: float32 [128, 4096], P(None, ('row', 'col'))
- step_bias_grad: float32 [4096], P(('row', 'col'))
- decay_log_grad: float32 [4096, 16], P(('row', 'col'))
- skip_gain_grad: float32 [4096], P(('row', 'col'))
- mixer_out_grad: float32 [4096, 2048], P('row', 'col')
- feed_norm_grad: float32 [2048], P('col')
- feed_gate_grad: float32 [2048, 8192], P('col', 'row')
- feed_up_grad: float32 [2048, 8192], P('col', 'row')
- feed_down_grad: float32 [8192, 2048], P('row', 'col')
The draws below stay inside these ranges and needn't reach their ends.
All inputs are finite; a program needn't handle non-finite values.
Results may differ from the reference program's by a relative error of at most 0.02.
The reference program's roundings to bfloat16 on the way count: a program that leaves them out, or rounds other values in their place, can miss the bound.
Values may be sent and summed in bfloat16 or wider, within the bound.
No kernel may reach another device: no remote copies, remote signals or barrier semaphores. Data moves between devices by JAX's collectives and lax.ppermute only.
A program may use at most 384 MiB of HBM per device.

```python
import jax
import jax.numpy as jnp
from jax import lax

D = 2048
INNER = 4096
STATE = 16
CONV = 4
DT_RANK = 128
FF = 8192
SEQ_LEN = 2048
SCAN_BLOCK = 16
TOKENS = 4096


def level_of(key, extent, shards, smallest, largest):
    def one(position, blocks):
        heights = jax.random.uniform(jax.random.fold_in(jax.random.fold_in(key, 6), position), (blocks,), jnp.float32, smallest / len(shards), largest / len(shards))
        return jnp.repeat(jnp.exp(heights), extent[position] // blocks).reshape((-1,) + (1,) * (len(extent) - position - 1))

    factor_of = one(*shards[0])
    for cut in shards[1:]:
        factor_of = factor_of * one(*cut)
    return factor_of


def scatter_about(key, extent, width, limit, cuts=(), kind=jnp.bfloat16):
    array = width * jax.random.normal(key, extent, jnp.float32)
    if cuts:
        array = array * level_of(key, extent, cuts, -0.22, 0.18)
    return jnp.clip(array, -limit, limit).astype(kind)


def setup_inputs(seed: int = 0) -> dict:
    key_list = jax.random.split(jax.random.key(seed), 18)
    return {
        "tokens": scatter_about(key_list[0], (TOKENS, D), 1.0, 6.0, ((0, 8), (1, 4))),
        "mixer_norm": jnp.clip(1.0 + 0.18 * jax.random.normal(key_list[1], (D,), jnp.float32), 0.1, 1.9),
        "in_value": scatter_about(key_list[2], (D, INNER), D ** -0.5, 0.125, ((0, 4), (1, 4)), jnp.float32),
        "in_gate": scatter_about(key_list[3], (D, INNER), D ** -0.5, 0.125, ((0, 4), (1, 4)), jnp.float32),
        "conv_weight": scatter_about(key_list[4], (INNER, CONV), CONV ** -0.5, 3.0, ((0, 16),), jnp.float32),
        "conv_bias": scatter_about(key_list[5], (INNER,), 0.3, 4.0, ((0, 16),), jnp.float32),
        "state_proj": scatter_about(key_list[6], (INNER, DT_RANK + 2 * STATE), (INNER // 8) ** -0.5, 0.25, ((0, 16),), jnp.float32),
        "step_proj": scatter_about(key_list[7], (DT_RANK, INNER), DT_RANK ** -0.5, 0.5, ((1, 16),), jnp.float32),
        "step_bias": jnp.clip(-5.0 + 3.0 * jax.random.uniform(key_list[8], (INNER,), jnp.float32) ** level_of(key_list[8], (INNER,), ((0, 16),), -0.2, 0.2), -5.0, -2.0),
        "decay_log": jnp.clip(2.8 * jax.random.uniform(key_list[9], (INNER, STATE), jnp.float32) ** level_of(key_list[9], (INNER, STATE), ((0, 16),), -0.2, 0.2), 0.0, 2.8),
        "skip_gain": jnp.clip(0.5 + 1.0 * jax.random.uniform(key_list[10], (INNER,), jnp.float32) ** level_of(key_list[10], (INNER,), ((0, 16),), -0.2, 0.2), 0.5, 1.5),
        "mixer_out": scatter_about(key_list[11], (INNER, D), (INNER // 4) ** -0.5, 0.1875, ((0, 4), (1, 4)), jnp.float32),
        "feed_norm": jnp.clip(1.0 + 0.18 * jax.random.normal(key_list[12], (D,), jnp.float32), 0.1, 1.9),
        "feed_gate": scatter_about(key_list[13], (D, FF), D ** -0.5, 0.125, ((0, 4), (1, 4)), jnp.float32),
        "feed_up": scatter_about(key_list[14], (D, FF), D ** -0.5, 0.125, ((0, 4), (1, 4)), jnp.float32),
        "feed_down": scatter_about(key_list[15], (FF, D), (FF // 2) ** -0.5, 0.09375, ((0, 4), (1, 4)), jnp.float32),
        "out_grad": scatter_about(key_list[16], (TOKENS, D), 1.0, 6.0, ((0, 8), (1, 4))),
    }


@jax.custom_vjp
def low(v):
    return lax.optimization_barrier(v.astype(jnp.bfloat16)).astype(jnp.float32)

@jax.custom_vjp
def low_back(v):
    return v

def low_keep(v):
    return (low(v), None)

def low_pass(kept, grad):
    return (grad,)

def back_keep(v):
    return (v, None)

def back_low(kept, grad):
    return (low(grad),)
low.defvjp(low_keep, low_pass)
low_back.defvjp(back_keep, back_low)
epsilon = 1e-05

def matmul(multiplicand, multiplier):
    return jnp.dot(multiplicand, multiplier, precision=lax.Precision.HIGHEST, preferred_element_type=jnp.float32)

def sigmoid_linear(values):
    return values * jax.nn.sigmoid(values)

def rms_scaled(values, weights):
    inverse = lax.rsqrt(lax.optimization_barrier(jnp.mean(values * values, axis=1, keepdims=True)) + epsilon)
    return values * inverse * weights[None, :]

def causal_conv(values, weights, biases):
    padded = jnp.pad(values, ((CONV - 1, 0), (0, 0)))
    summed = jnp.zeros(values.shape, jnp.float32) + biases[None, :]
    for offset in range(CONV):
        summed = summed + padded[offset:offset + SEQ_LEN] * weights[:, offset][None, :]
    return summed

def recurrence(step_size, conv_act, in_coef, out_coef, decay_rate):
    block_count = SEQ_LEN // SCAN_BLOCK

    def token_step(memory, inputs):
        step_now, act_now, in_now, out_now = inputs
        memory = jnp.exp(step_now[:, None] * decay_rate) * memory + (step_now * act_now)[:, None] * in_now[None, :]
        return (memory, lax.optimization_barrier(jnp.sum(memory * out_now[None, :], axis=1)))

    @jax.checkpoint
    def block_step(memory, inputs):
        return lax.scan(token_step, memory, inputs)
    blocked = tuple((values.reshape((block_count, SCAN_BLOCK) + values.shape[1:]) for values in (step_size, conv_act, in_coef, out_coef)))
    memory = jnp.zeros(decay_rate.shape, jnp.float32)
    _, outputs = lax.scan(block_step, memory, blocked)
    return outputs.reshape(step_size.shape)

def block_forward(parameters, inputs):
    mixer_norm, in_value, in_gate, conv_weight, conv_bias, state_proj, step_proj, step_bias, decay_log, skip_gain, mixer_out, feed_norm, feed_gate, feed_up, feed_down = parameters
    normed = low(rms_scaled(inputs, mixer_norm))
    mixer_in = low_back(matmul(normed, low(in_value)))
    gate_in = low_back(matmul(normed, low(in_gate)))
    conv_out = causal_conv(mixer_in, conv_weight, conv_bias)
    conv_act = low(sigmoid_linear(conv_out))
    projected = low_back(matmul(conv_act, low(state_proj)))
    step_low = low(projected[:, :DT_RANK])
    in_coef = projected[:, DT_RANK:DT_RANK + STATE]
    out_coef = projected[:, DT_RANK + STATE:]
    step_size = jax.nn.softplus(low_back(matmul(step_low, low(step_proj))) + step_bias[None, :])
    scan_out = recurrence(step_size, conv_act, in_coef, out_coef, -jnp.exp(decay_log)) + skip_gain[None, :] * conv_act
    gated = low(scan_out * sigmoid_linear(gate_in))
    middle = inputs + low_back(matmul(gated, low(mixer_out)))
    normed_feed = low(rms_scaled(middle, feed_norm))
    gate_pre = low_back(matmul(normed_feed, low(feed_gate)))
    up_pre = low_back(matmul(normed_feed, low(feed_up)))
    hidden = low(sigmoid_linear(gate_pre) * up_pre)
    return middle + low_back(matmul(hidden, low(feed_down)))

def reference(tokens, mixer_norm, in_value, in_gate, conv_weight, conv_bias, state_proj, step_proj, step_bias, decay_log, skip_gain, mixer_out, feed_norm, feed_gate, feed_up, feed_down, out_grad):
    parameters = (mixer_norm, in_value, in_gate, conv_weight, conv_bias, state_proj, step_proj, step_bias, decay_log, skip_gain, mixer_out, feed_norm, feed_gate, feed_up, feed_down)
    sequences = TOKENS // SEQ_LEN
    inputs = tokens.astype(jnp.float32).reshape(sequences, SEQ_LEN, D)
    cotangent = out_grad.astype(jnp.float32).reshape(sequences, SEQ_LEN, D)

    def one_sequence(accumulated, sequence_data):
        values, upstream = sequence_data
        result, pullback = jax.vjp(block_forward, parameters, values)
        grad_params, grad_values = pullback(upstream)
        accumulated = jax.tree.map(lambda earlier, addition: earlier + addition, accumulated, grad_params)
        return (accumulated, (result.astype(jnp.bfloat16), grad_values))
    zeroes = jax.tree.map(jnp.zeros_like, parameters)
    summed, (results, grad_tokens) = lax.scan(one_sequence, zeroes, (inputs, cotangent))
    return (results.reshape(TOKENS, D), grad_tokens.reshape(TOKENS, D), summed[0], summed[1], summed[2], summed[3], summed[4], summed[5], summed[6], summed[7], summed[8], summed[9], summed[10], summed[11], summed[12], summed[13], summed[14])
```

```python
import jax
import jax.numpy as jnp
import numpy as np
from jax import lax
from jax.experimental import pallas as pl
from jax.experimental.pallas import tpu as pltpu
from jax.sharding import PartitionSpec as P

STATE = 16
CONV = 4
DT_RANK = 128
LANES = 128
ROWS = 8
LOG2E = np.float32(np.log2(np.e))
LN2 = np.float32(np.log(2.0))

epsilon = 1e-05
contract_first = (((0,), (0,)), ((), ()))
contract_last = (((1,), (1,)), ((), ()))
contract_inner = (((1,), (0,)), ((), ()))


def sigmoid_linear(values):
    return values * jax.nn.sigmoid(values)


def sigmoid_slope(values):
    logistic = jax.nn.sigmoid(values)
    return logistic * (1.0 + values * (1.0 - logistic))


def product(multiplicand, multiplier, dims=contract_inner):
    return lax.dot_general(multiplicand, multiplier, dims, preferred_element_type=jnp.float32)


def low(values):
    return values.astype(jnp.bfloat16)


def swap(values, axis, distance):
    return lax.ppermute(
        values, axis, [(i, i ^ distance) for i in range(lax.axis_size(axis))]
    )


def shift(values, axis, distance):
    size = lax.axis_size(axis)
    pairs = [(i, i + distance) for i in range(size) if 0 <= i + distance < size]
    return lax.ppermute(values, axis, pairs)


def gather_by_swaps(values, axis_name, axis):
    size, length = lax.axis_size(axis_name), values.shape[axis]
    index = lax.axis_index(axis_name)
    shape = list(values.shape)
    shape[axis] = size * length
    joined = jnp.zeros(shape, values.dtype)
    for distance in range(size):
        part = swap(values, axis_name, distance) if distance else values
        joined = lax.dynamic_update_slice_in_dim(
            joined, part, (index ^ distance) * length, axis
        )
    return joined


def scatter_by_swaps(values, axis_name, axis, dtype):
    size = lax.axis_size(axis_name)
    length = values.shape[axis] // size
    index = lax.axis_index(axis_name)

    def block(distance):
        return lax.dynamic_slice_in_dim(values, (index ^ distance) * length, length, axis)

    total = block(0).astype(jnp.float32)
    for distance in range(1, size):
        total = total + swap(block(distance).astype(dtype), axis_name, distance).astype(
            jnp.float32
        )
    return total


def row_gather(values):
    if lax.axis_size("row") == 4:
        return gather_by_swaps(values, "row", 0)
    return lax.all_gather(values, "row", axis=0, tiled=True)


def row_scatter(values):
    if lax.axis_size("row") == 4:
        return scatter_by_swaps(values, "row", 0, jnp.bfloat16)
    return lax.psum_scatter(low(values), "row", scatter_dimension=0, tiled=True).astype(
        jnp.float32
    )


def row_total(values):
    if lax.axis_size("row") == 4:
        total = values
        for distance in range(1, 4):
            total = total + swap(values, "row", distance)
        return total
    return lax.psum(values, "row")


def block_moves():
    rows, cols = lax.axis_size("row"), lax.axis_size("col")
    return [(k, (k % rows) * cols + k // rows) for k in range(rows * cols)]


def to_whole_features(values):
    split = lax.all_to_all(values, "col", split_axis=0, concat_axis=1, tiled=True)
    return lax.ppermute(split, ("row", "col"), block_moves())


def to_feature_blocks(values):
    back = [(target, source) for source, target in block_moves()]
    split = lax.ppermute(values, ("row", "col"), back)
    return lax.all_to_all(split, "col", split_axis=1, concat_axis=0, tiled=True)


def gather_weight(weight, axis):
    half = weight.shape[axis] // lax.axis_size("dp")
    part = lax.dynamic_slice_in_dim(weight, lax.axis_index("dp") * half, half, axis)
    return lax.all_gather(low(part), ("col", "dp"), axis=axis, tiled=True)


def scatter_gradient(gradient, axis):
    own = lax.psum_scatter(
        low(gradient), ("col", "dp"), scatter_dimension=axis, tiled=True
    )
    other = swap(own, "dp", 1)
    first = lax.axis_index("dp") == 0
    return jnp.concatenate(
        [jnp.where(first, own, other), jnp.where(first, other, own)], axis=axis
    ).astype(jnp.float32)


def fold_rows(parts):
    row = lax.broadcasted_iota(jnp.int32, parts[0].shape, 0)
    for half in (1, 2, 4):
        mask = (row & half) == 0
        parts = [
            jnp.where(mask, a, b) + pltpu.roll(jnp.where(mask, b, a), ROWS - half, 0)
            for a, b in zip(parts[0::2], parts[1::2])
        ]
    return parts[0]


def spread(ref, token):
    return ref[pl.ds(token, ROWS, stride=0), :]


class Tiling:
    def __init__(self, tokens, channels, backward):
        groups = channels // LANES
        self.tokens, self.channels = tokens, channels
        self.per = min(8, groups)
        self.block = min(128, tokens)
        self.blocks = tokens // self.block
        self.grid = (groups // self.per, self.blocks)
        self.width = self.per * LANES
        self.backward = backward
        self.lanes = [slice(g * LANES, (g + 1) * LANES) for g in range(self.per)]

    def at(self, b):
        return self.blocks - 1 - b if self.backward else b

    def narrow(self):
        def spec(i):
            return pl.BlockSpec(
                (self.block, LANES), lambda g, b: (self.at(b), g * self.per + i)
            )

        return [spec(i) for i in range(self.per)]

    def token_spec(self):
        return pl.BlockSpec((self.block, self.width), lambda g, b: (self.at(b), g))

    def wide_spec(self):
        return pl.BlockSpec((self.block, STATE, LANES), lambda g, b: (self.at(b), 0, 0))

    def state_spec(self):
        return pl.BlockSpec((STATE, self.width), lambda g, b: (0, g))

    def history_spec(self):
        return pl.BlockSpec((self.block, STATE, self.width), lambda g, b: (self.at(b), 0, g))

    def part_spec(self):
        return pl.BlockSpec(
            (1, self.block, STATE, LANES), lambda g, b: (g, self.at(b), 0, 0)
        )

    def load(self, ref):
        out = []
        for lanes in self.lanes:
            out += [ref[0:8, lanes], ref[8:16, lanes]]
        return tuple(out)

    def store(self, ref, values):
        for g, lanes in enumerate(self.lanes):
            ref[0:8, lanes] = values[2 * g]
            ref[8:16, lanes] = values[2 * g + 1]

    def call(self, kernel, name, in_specs, out_specs, out_shape, scratch=()):
        return pl.pallas_call(
            kernel,
            out_shape=out_shape,
            grid=self.grid,
            in_specs=in_specs,
            out_specs=out_specs,
            scratch_shapes=list(scratch),
            compiler_params=pltpu.CompilerParams(
                dimension_semantics=("arbitrary", "arbitrary"),
                vmem_limit_bytes=56 * 2**20,
            ),
            name=name,
        )


def pair(ref, token):
    return ref[token, 0:8, :], ref[token, 8:16, :]


def f32(*shape):
    return jax.ShapeDtypeStruct(shape, jnp.float32)


def chunk_state(step, drive, wide, rate, backward):
    t = Tiling(*step.shape, backward)
    per = t.per

    def kernel(*refs):
        step_refs, drive_refs = refs[:per], refs[per : 2 * per]
        wide_ref, rate_ref, state_ref = refs[2 * per :]

        @pl.when(pl.program_id(1) == 0)
        def _():
            state_ref[...] = jnp.zeros_like(state_ref)

        rates = t.load(rate_ref)

        def some(i, state):
            state = list(state)
            base = t.block - ROWS - i * ROWS if backward else i * ROWS
            for j in range(ROWS - 1, -1, -1) if backward else range(ROWS):
                token = base + j
                wides = pair(wide_ref, token)
                for g in range(per):
                    now = spread(step_refs[g], token)
                    force = spread(drive_refs[g], token)
                    for k in (0, 1):
                        m = 2 * g + k
                        factor = jnp.exp2(now * rates[m])
                        if backward:
                            state[m] = factor * (state[m] + force * wides[k])
                        else:
                            state[m] = factor * state[m] + force * wides[k]
            return tuple(state)

        t.store(
            state_ref, lax.fori_loop(0, t.block // ROWS, some, t.load(state_ref))
        )

    return t.call(
        kernel,
        "chunk_state_back" if backward else "chunk_state",
        t.narrow() + t.narrow() + [t.wide_spec(), t.state_spec()],
        t.state_spec(),
        f32(STATE, t.channels),
    )(*[step] * per, *[drive] * per, wide, rate)


def scan_forward(step, drive, in_wide, out_wide, rate, entry):
    t = Tiling(*step.shape, False)
    per = t.per

    def kernel(*refs):
        step_refs, drive_refs = refs[:per], refs[per : 2 * per]
        in_ref, out_ref, rate_ref, entry_ref, y_ref, before_ref, last_ref = refs[2 * per :]

        @pl.when(pl.program_id(1) == 0)
        def _():
            last_ref[...] = entry_ref[...]

        rates = t.load(rate_ref)

        def some(i, state):
            state = list(state)
            base = pl.multiple_of(i * ROWS, ROWS)
            sums = [[None] * ROWS for _ in range(per)]
            for j in range(ROWS):
                token = base + j
                ins, outs = pair(in_ref, token), pair(out_ref, token)
                for g in range(per):
                    now = spread(step_refs[g], token)
                    force = spread(drive_refs[g], token)
                    total = None
                    for k in (0, 1):
                        m = 2 * g + k
                        before_ref[token, 8 * k : 8 * k + 8, t.lanes[g]] = state[m]
                        state[m] = jnp.exp2(now * rates[m]) * state[m] + force * ins[k]
                        term = state[m] * outs[k]
                        total = term if total is None else total + term
                    sums[g][j] = total
            for g in range(per):
                y_ref[pl.ds(base, ROWS), t.lanes[g]] = fold_rows(sums[g])
            return tuple(state)

        t.store(last_ref, lax.fori_loop(0, t.block // ROWS, some, t.load(last_ref)))

    return t.call(
        kernel,
        "scan_forward",
        t.narrow()
        + t.narrow()
        + [t.wide_spec(), t.wide_spec(), t.state_spec(), t.state_spec()],
        (t.token_spec(), t.history_spec(), t.state_spec()),
        (
            f32(t.tokens, t.channels),
            f32(t.tokens, STATE, t.channels),
            f32(STATE, t.channels),
        ),
    )(*[step] * per, *[drive] * per, in_wide, out_wide, rate, entry)


def scan_backward(step, drive, back, in_wide, out_wide, rate, entry, before, last):
    t = Tiling(*step.shape, True)
    per = t.per

    def kernel(*refs):
        step_refs, drive_refs, back_refs = (refs[i * per : (i + 1) * per] for i in range(3))
        in_ref, out_ref, rate_ref, entry_ref, before_ref, last_ref = refs[
            3 * per : 3 * per + 6
        ]
        rate_sum_ref, in_sum_ref, decay_ref, in_part_ref, out_part_ref = refs[
            3 * per + 6 : 3 * per + 11
        ]
        carry_ref, state_ref = refs[3 * per + 11 :]

        @pl.when(pl.program_id(1) == 0)
        def _():
            decay_ref[...] = jnp.zeros_like(decay_ref)
            carry_ref[...] = entry_ref[...]
            state_ref[...] = last_ref[...]

        rates = t.load(rate_ref)

        def some(i, carried):
            carry, state, decay = (list(part) for part in carried)
            base = pl.multiple_of(t.block - ROWS - i * ROWS, ROWS)
            rate_sums = [[None] * ROWS for _ in range(per)]
            in_sums = [[None] * ROWS for _ in range(per)]
            for j in range(ROWS - 1, -1, -1):
                token = base + j
                ins, outs = pair(in_ref, token), pair(out_ref, token)
                in_part, out_part = [None, None], [None, None]
                for g in range(per):
                    now = spread(step_refs[g], token)
                    force = spread(drive_refs[g], token)
                    above = spread(back_refs[g], token)
                    by_rate, by_in = [None, None], [None, None]
                    for k in (0, 1):
                        m = 2 * g + k
                        earlier = before_ref[token, 8 * k : 8 * k + 8, t.lanes[g]]
                        grad = carry[m] + above * outs[k]
                        carry[m] = jnp.exp2(now * rates[m]) * grad
                        weighted = carry[m] * earlier
                        decay[m] = decay[m] + weighted * now
                        by_rate[k] = weighted * rates[m]
                        by_in[k] = grad * ins[k]
                        for parts, term in (
                            (in_part, grad * force),
                            (out_part, above * state[m]),
                        ):
                            parts[k] = term if parts[k] is None else parts[k] + term
                        state[m] = earlier
                    rate_sums[g][j] = by_rate[0] + by_rate[1]
                    in_sums[g][j] = by_in[0] + by_in[1]
                for k in (0, 1):
                    in_part_ref[0, token, 8 * k : 8 * k + 8, :] = in_part[k]
                    out_part_ref[0, token, 8 * k : 8 * k + 8, :] = out_part[k]
            for g in range(per):
                rate_sum_ref[pl.ds(base, ROWS), t.lanes[g]] = fold_rows(rate_sums[g])
                in_sum_ref[pl.ds(base, ROWS), t.lanes[g]] = fold_rows(in_sums[g])
            return tuple(carry), tuple(state), tuple(decay)

        carry, state, decay = lax.fori_loop(
            0,
            t.block // ROWS,
            some,
            (t.load(carry_ref), t.load(state_ref), t.load(decay_ref)),
        )
        t.store(carry_ref, carry)
        t.store(state_ref, state)
        t.store(decay_ref, decay)

    parts = f32(t.grid[0], t.tokens, STATE, LANES)
    rate_sum, in_sum, decay, in_part, out_part = t.call(
        kernel,
        "scan_backward",
        t.narrow()
        + t.narrow()
        + t.narrow()
        + [
            t.wide_spec(),
            t.wide_spec(),
            t.state_spec(),
            t.state_spec(),
            t.history_spec(),
            t.state_spec(),
        ],
        (t.token_spec(), t.token_spec(), t.state_spec(), t.part_spec(), t.part_spec()),
        (
            f32(t.tokens, t.channels),
            f32(t.tokens, t.channels),
            f32(STATE, t.channels),
            parts,
            parts,
        ),
        [pltpu.VMEM((STATE, t.width), jnp.float32)] * 2,
    )(
        *[step] * per,
        *[drive] * per,
        *[back] * per,
        in_wide,
        out_wide,
        rate,
        entry,
        before,
        last,
    )
    return rate_sum, in_sum, decay, jnp.sum(in_part, (0, 3)), jnp.sum(out_part, (0, 3))


def chunk_entry(state, step_total, rate, direction):
    packed = jnp.concatenate([state, step_total], axis=0)
    entry = None
    for distance in range(lax.axis_size("col") - 1, 0, -1):
        got = shift(packed, "col", direction * distance)
        if entry is None:
            entry = got[:STATE]
        else:
            entry = got[:STATE] + jnp.exp2(got[STATE:] * rate) * entry
    return entry


def widen(coefficients):
    return jnp.broadcast_to(coefficients[:, :, None], coefficients.shape + (LANES,))


def norm_forward(values, weights):
    inverse = lax.rsqrt(jnp.mean(values * values, axis=1, keepdims=True) + epsilon)
    scaled = values * inverse
    return scaled, inverse, low(scaled * weights)


def norm_backward(upstream, scaled, inverse, weights):
    weighted = upstream * weights
    inner_mean = jnp.mean(weighted * scaled, axis=1, keepdims=True)
    return (
        inverse * (weighted - scaled * inner_mean),
        jnp.sum(upstream * scaled, axis=0, keepdims=True),
    )


def body(
    tokens,
    mixer_norm,
    in_value,
    in_gate,
    conv_weight,
    conv_bias,
    state_proj,
    step_proj,
    step_bias,
    decay_log,
    skip_gain,
    mixer_out,
    feed_norm,
    feed_gate,
    feed_up,
    feed_down,
    out_grad,
):
    value_low = gather_weight(in_value, 0)
    gate_low = gather_weight(in_gate, 0)
    mixer_low = gather_weight(mixer_out, 1)
    feed_gate_low = gather_weight(feed_gate, 0)
    feed_up_low = gather_weight(feed_up, 0)
    feed_down_low = gather_weight(feed_down, 1)

    inputs = to_whole_features(tokens).astype(jnp.float32)
    out_back_low = to_whole_features(out_grad)
    gains = gather_by_swaps(jnp.stack([mixer_norm, feed_norm]), "col", 1)
    mixer_gain, feed_gain = gains[0:1], gains[1:2]
    packed = jnp.concatenate(
        [
            conv_weight.T,
            conv_bias[None],
            step_bias[None],
            skip_gain[None],
            decay_log.T,
        ],
        axis=0,
    )
    packed = gather_by_swaps(packed, "col", 1)
    taps = packed[:CONV]
    conv_bias_row, step_bias_row, skip_row = (
        packed[CONV + i : CONV + i + 1] for i in range(3)
    )
    decay_rate = -jnp.exp(packed[CONV + 3 :])
    state_low = gather_by_swaps(low(state_proj), "col", 0)
    step_weight = gather_by_swaps(low(step_proj), "col", 1)

    scaled_first, inverse_first, normed_first = norm_forward(inputs, mixer_gain)
    normed_all = row_gather(normed_first)
    grad_all = row_gather(out_back_low)
    mixer_in = product(normed_all, value_low)
    gate_in = product(normed_all, gate_low)
    count = mixer_in.shape[0]
    earlier = shift(mixer_in[-ROWS:], "col", 1)
    padded = jnp.concatenate([earlier[ROWS - CONV + 1 :], mixer_in], axis=0)
    conv_out = conv_bias_row + sum(
        padded[k : k + count] * taps[k : k + 1] for k in range(CONV)
    )
    conv_act = low(sigmoid_linear(conv_out))
    projected = row_total(product(conv_act, state_low))
    step_low = low(projected[:, :DT_RANK])
    in_wide = widen(projected[:, DT_RANK : DT_RANK + STATE])
    out_wide = widen(projected[:, DT_RANK + STATE :])
    step_pre = product(step_low, step_weight) + step_bias_row
    step_size = jax.nn.softplus(step_pre)
    act_float = conv_act.astype(jnp.float32)
    drive = step_size * act_float
    rate = decay_rate * LOG2E
    step_total = jnp.sum(step_size, axis=0, keepdims=True)
    handed = chunk_state(step_size, drive, in_wide, rate, False)
    entry = chunk_entry(handed, step_total, rate, 1)
    scanned, before, last = scan_forward(step_size, drive, in_wide, out_wide, rate, entry)
    scan_out = scanned + skip_row * act_float
    gate_act = sigmoid_linear(gate_in)
    gated = low(scan_out * gate_act)
    middle = inputs + row_scatter(product(gated, mixer_low))

    scaled_second, inverse_second, normed_second = norm_forward(middle, feed_gain)
    normed_feed = row_gather(normed_second)
    gate_pre = product(normed_feed, feed_gate_low)
    up_pre = product(normed_feed, feed_up_low)
    gate_swish = sigmoid_linear(gate_pre)
    hidden = low(gate_swish * up_pre)
    output = to_feature_blocks(low(middle + row_scatter(product(hidden, feed_down_low))))

    feed_down_grad = scatter_gradient(product(hidden, grad_all, contract_first), 1)
    hidden_back = product(grad_all, feed_down_low, contract_last)
    gate_back = low(hidden_back * up_pre * sigmoid_slope(gate_pre))
    up_back = low(hidden_back * gate_swish)
    feed_gate_grad = scatter_gradient(product(normed_feed, gate_back, contract_first), 0)
    feed_up_grad = scatter_gradient(product(normed_feed, up_back, contract_first), 0)
    normed_back = row_scatter(
        product(gate_back, feed_gate_low, contract_last)
        + product(up_back, feed_up_low, contract_last)
    )
    middle_norm, feed_norm_part = norm_backward(
        normed_back, scaled_second, inverse_second, feed_gain
    )
    middle_back = out_back_low.astype(jnp.float32) + middle_norm
    middle_all = row_gather(low(middle_back))

    mixer_out_grad = scatter_gradient(product(gated, middle_all, contract_first), 1)
    gated_back = product(middle_all, mixer_low, contract_last)
    scan_back = gated_back * gate_act
    gate_in_back = low(gated_back * scan_out * sigmoid_slope(gate_in))
    in_gate_grad = scatter_gradient(product(normed_all, gate_in_back, contract_first), 0)
    handed_back = chunk_state(step_size, scan_back, out_wide, rate, True)
    entry_back = chunk_entry(handed_back, step_total, rate, -1)
    rate_sum, in_sum, decay_sum, in_back, out_back = scan_backward(
        step_size, drive, scan_back, in_wide, out_wide, rate, entry_back, before, last
    )
    step_back = rate_sum * LN2 + act_float * in_sum
    act_scan = step_size * in_sum + skip_row * scan_back
    pre_back = step_back * jax.nn.sigmoid(step_pre)
    pre_low = low(pre_back)
    rank_back = product(pre_low, step_weight, contract_last)
    proj_back = low(row_total(jnp.concatenate([rank_back, in_back, out_back], axis=1)))
    act_back = act_scan + product(proj_back, state_low, contract_last)
    conv_back = act_back * sigmoid_slope(conv_out)
    later = shift(conv_back[:ROWS], "col", -1)
    trailing = jnp.concatenate([conv_back, later[: CONV - 1]], axis=0)
    mixer_back = low(
        sum(
            trailing[CONV - 1 - k : CONV - 1 - k + count] * taps[k : k + 1]
            for k in range(CONV)
        )
    )
    in_value_grad = scatter_gradient(product(normed_all, mixer_back, contract_first), 0)
    normed_first_back = row_scatter(
        product(mixer_back, value_low, contract_last)
        + product(gate_in_back, gate_low, contract_last)
    )
    input_norm, mixer_norm_part = norm_backward(
        normed_first_back, scaled_first, inverse_first, mixer_gain
    )
    tokens_grad = to_feature_blocks(low(middle_back + input_norm)).astype(jnp.float32)

    def over_tokens(values):
        return jnp.sum(values, axis=0, keepdims=True)

    packed_grad = jnp.concatenate(
        [over_tokens(conv_back * padded[k : k + count]) for k in range(CONV)]
        + [
            over_tokens(conv_back),
            over_tokens(pre_back),
            over_tokens(scan_back * act_float),
            decay_sum * decay_rate,
        ],
        axis=0,
    )

    def over_group(values, axis, dtype):
        own = scatter_by_swaps(values, "col", axis, dtype)
        return own + swap(own, "dp", 1)

    packed_grad = over_group(packed_grad, 1, jnp.float32)
    state_proj_grad = over_group(
        product(conv_act, proj_back, contract_first), 0, jnp.bfloat16
    )
    step_proj_grad = over_group(product(step_low, pre_low, contract_first), 1, jnp.bfloat16)
    gain_sums = scatter_by_swaps(
        jnp.concatenate([mixer_norm_part, feed_norm_part], axis=0), "col", 1, jnp.float32
    )
    gain_sums = lax.psum(gain_sums, ("dp", "row"))
    return (
        output,
        tokens_grad,
        gain_sums[0],
        in_value_grad,
        in_gate_grad,
        packed_grad[:CONV].T,
        packed_grad[CONV],
        state_proj_grad,
        step_proj_grad,
        packed_grad[CONV + 1],
        packed_grad[CONV + 3 :].T,
        packed_grad[CONV + 2],
        mixer_out_grad,
        gain_sums[1],
        feed_gate_grad,
        feed_up_grad,
        feed_down_grad,
    )


def solution(mesh):
    token_spec = P(("dp", "row"), "col")
    weight_in, weight_out = P("col", "row"), P("row", "col")
    channel, channel_rows = P(("row", "col")), P(("row", "col"), None)
    parameters = (
        P("col"),
        weight_in,
        weight_in,
        channel_rows,
        channel,
        channel_rows,
        P(None, ("row", "col")),
        channel,
        channel_rows,
        channel,
        weight_out,
        P("col"),
        weight_in,
        weight_in,
        weight_out,
    )
    return jax.shard_map(
        body,
        mesh=mesh,
        in_specs=(token_spec,) + parameters + (token_spec,),
        out_specs=(token_spec, token_spec) + parameters,
        check_vma=False,
    )
```

```python
import jax
import jax.numpy as jnp
import numpy as np
from jax import lax
from jax.experimental import pallas as pl
from jax.experimental.pallas import tpu as pltpu
from jax.sharding import PartitionSpec as P

STATE = 16
CONV = 4
DT_RANK = 128
LANES = 128
ROWS = 8
LOG2E = np.float32(np.log2(np.e))
LN2 = np.float32(np.log(2.0))

epsilon = 1e-05
contract_first = (((0,), (0,)), ((), ()))
contract_last = (((1,), (1,)), ((), ()))
contract_inner = (((1,), (0,)), ((), ()))


def sigmoid_linear(values):
    return values * jax.nn.sigmoid(values)


def sigmoid_slope(values):
    logistic = jax.nn.sigmoid(values)
    return logistic * (1.0 + values * (1.0 - logistic))


def product(multiplicand, multiplier, dims=contract_inner):
    return lax.dot_general(multiplicand, multiplier, dims, preferred_element_type=jnp.float32)


def low(values):
    return values.astype(jnp.bfloat16)


def swap(values, axis, distance):
    return lax.ppermute(
        values, axis, [(i, i ^ distance) for i in range(lax.axis_size(axis))]
    )


def shift(values, axis, distance):
    size = lax.axis_size(axis)
    pairs = [(i, i + distance) for i in range(size) if 0 <= i + distance < size]
    return lax.ppermute(values, axis, pairs)


def gather_by_swaps(values, axis_name, axis):
    size, length = lax.axis_size(axis_name), values.shape[axis]
    index = lax.axis_index(axis_name)
    shape = list(values.shape)
    shape[axis] = size * length
    joined = jnp.zeros(shape, values.dtype)
    for distance in range(size):
        part = swap(values, axis_name, distance) if distance else values
        joined = lax.dynamic_update_slice_in_dim(
            joined, part, (index ^ distance) * length, axis
        )
    return joined


def scatter_by_swaps(values, axis_name, axis, dtype):
    size = lax.axis_size(axis_name)
    length = values.shape[axis] // size
    index = lax.axis_index(axis_name)

    def block(distance):
        return lax.dynamic_slice_in_dim(values, (index ^ distance) * length, length, axis)

    total = block(0).astype(jnp.float32)
    for distance in range(1, size):
        total = total + swap(block(distance).astype(dtype), axis_name, distance).astype(
            jnp.float32
        )
    return total


def row_gather(values):
    if lax.axis_size("row") == 4:
        return gather_by_swaps(values, "row", 0)
    return lax.all_gather(values, "row", axis=0, tiled=True)


def row_scatter(values):
    if lax.axis_size("row") == 4:
        return scatter_by_swaps(values, "row", 0, jnp.bfloat16)
    return lax.psum_scatter(low(values), "row", scatter_dimension=0, tiled=True).astype(
        jnp.float32
    )


def row_total(values):
    if lax.axis_size("row") == 4:
        total = values
        for distance in range(1, 4):
            total = total + swap(values, "row", distance)
        return total
    return lax.psum(values, "row")


def block_moves():
    rows, cols = lax.axis_size("row"), lax.axis_size("col")
    return [(k, (k % rows) * cols + k // rows) for k in range(rows * cols)]


def exchange(pieces, axis_name):
    index = lax.axis_index(axis_name)
    joined = jnp.zeros_like(pieces)
    for distance in range(lax.axis_size(axis_name)):
        part = lax.dynamic_slice_in_dim(pieces, index ^ distance, 1, 0)
        if distance:
            part = swap(part, axis_name, distance)
        joined = lax.dynamic_update_slice_in_dim(joined, part, index ^ distance, 0)
    return joined


def to_whole_features(values):
    rows, cols = lax.axis_size("row"), lax.axis_size("col")
    if rows == cols:
        count, features = values.shape
        pieces = values.reshape(rows, count // rows, features)
        pieces = exchange(exchange(pieces, "row"), "col")
        return jnp.concatenate([pieces[c] for c in range(cols)], axis=1)
    split = lax.all_to_all(values, "col", split_axis=0, concat_axis=1, tiled=True)
    return lax.ppermute(split, ("row", "col"), block_moves())


def to_feature_blocks(values):
    rows, cols = lax.axis_size("row"), lax.axis_size("col")
    if rows == cols:
        count, features = values.shape[0], values.shape[1] // cols
        pieces = jnp.stack([values[:, c * features : (c + 1) * features] for c in range(cols)])
        pieces = exchange(exchange(pieces, "col"), "row")
        return pieces.reshape(rows * count, features)
    back = [(target, source) for source, target in block_moves()]
    split = lax.ppermute(values, ("row", "col"), back)
    return lax.all_to_all(split, "col", split_axis=1, concat_axis=0, tiled=True)


def gather_weight(weight, axis):
    half = weight.shape[axis] // lax.axis_size("dp")
    part = lax.dynamic_slice_in_dim(weight, lax.axis_index("dp") * half, half, axis)
    return lax.all_gather(low(part), ("col", "dp"), axis=axis, tiled=True)


def scatter_gradient(gradient, axis, after=None):
    if after is not None:
        gradient, _ = lax.optimization_barrier((gradient, after))
    return lax.psum_scatter(gradient, ("col", "dp"), scatter_dimension=axis, tiled=True)


def both_halves(own, axis):
    other = swap(own, "dp", 1)
    first = lax.axis_index("dp") == 0
    return jnp.concatenate(
        [jnp.where(first, own, other), jnp.where(first, other, own)], axis=axis
    ).astype(jnp.float32)


def fold_rows(parts):
    row = lax.broadcasted_iota(jnp.int32, parts[0].shape, 0)
    for half in (1, 2, 4):
        mask = (row & half) == 0
        parts = [
            jnp.where(mask, a, b) + pltpu.roll(jnp.where(mask, b, a), ROWS - half, 0)
            for a, b in zip(parts[0::2], parts[1::2])
        ]
    return parts[0]


def spread(ref, token):
    return ref[pl.ds(token, ROWS, stride=0), :]


class Tiling:
    def __init__(self, tokens, channels, backward):
        groups = channels // LANES
        self.tokens, self.channels = tokens, channels
        self.per = min(8, groups)
        self.block = min(128, tokens)
        self.blocks = tokens // self.block
        self.grid = (groups // self.per, self.blocks)
        self.width = self.per * LANES
        self.backward = backward
        self.lanes = [slice(g * LANES, (g + 1) * LANES) for g in range(self.per)]

    def at(self, b):
        return self.blocks - 1 - b if self.backward else b

    def narrow(self):
        def spec(i):
            return pl.BlockSpec(
                (self.block, LANES), lambda g, b: (self.at(b), g * self.per + i)
            )

        return [spec(i) for i in range(self.per)]

    def token_spec(self):
        return pl.BlockSpec((self.block, self.width), lambda g, b: (self.at(b), g))

    def wide_spec(self):
        return pl.BlockSpec((self.block, STATE, LANES), lambda g, b: (self.at(b), 0, 0))

    def state_spec(self):
        return pl.BlockSpec((STATE, self.width), lambda g, b: (0, g))

    def history_spec(self):
        return pl.BlockSpec((self.block, STATE, self.width), lambda g, b: (self.at(b), 0, g))

    def part_spec(self):
        return pl.BlockSpec(
            (1, self.block, STATE, LANES), lambda g, b: (g, self.at(b), 0, 0)
        )

    def load(self, ref):
        out = []
        for lanes in self.lanes:
            out += [ref[0:8, lanes], ref[8:16, lanes]]
        return tuple(out)

    def store(self, ref, values):
        for g, lanes in enumerate(self.lanes):
            ref[0:8, lanes] = values[2 * g]
            ref[8:16, lanes] = values[2 * g + 1]

    def call(self, kernel, name, in_specs, out_specs, out_shape, scratch=()):
        return pl.pallas_call(
            kernel,
            out_shape=out_shape,
            grid=self.grid,
            in_specs=in_specs,
            out_specs=out_specs,
            scratch_shapes=list(scratch),
            compiler_params=pltpu.CompilerParams(
                dimension_semantics=("arbitrary", "arbitrary"),
                vmem_limit_bytes=56 * 2**20,
            ),
            name=name,
        )


def pair(ref, token):
    return ref[token, 0:8, :], ref[token, 8:16, :]


def f32(*shape):
    return jax.ShapeDtypeStruct(shape, jnp.float32)


def chunk_state(step, drive, wide, rate, backward):
    t = Tiling(*step.shape, backward)
    per = t.per

    def kernel(*refs):
        step_refs, drive_refs = refs[:per], refs[per : 2 * per]
        wide_ref, rate_ref, state_ref = refs[2 * per :]

        @pl.when(pl.program_id(1) == 0)
        def _():
            state_ref[...] = jnp.zeros_like(state_ref)

        rates = t.load(rate_ref)

        def some(i, state):
            state = list(state)
            base = t.block - ROWS - i * ROWS if backward else i * ROWS
            for j in range(ROWS - 1, -1, -1) if backward else range(ROWS):
                token = base + j
                wides = pair(wide_ref, token)
                for g in range(per):
                    now = spread(step_refs[g], token)
                    force = spread(drive_refs[g], token)
                    for k in (0, 1):
                        m = 2 * g + k
                        factor = jnp.exp2(now * rates[m])
                        if backward:
                            state[m] = factor * (state[m] + force * wides[k])
                        else:
                            state[m] = factor * state[m] + force * wides[k]
            return tuple(state)

        t.store(
            state_ref, lax.fori_loop(0, t.block // ROWS, some, t.load(state_ref))
        )

    return t.call(
        kernel,
        "chunk_state_back" if backward else "chunk_state",
        t.narrow() + t.narrow() + [t.wide_spec(), t.state_spec()],
        t.state_spec(),
        f32(STATE, t.channels),
    )(*[step] * per, *[drive] * per, wide, rate)


def scan_forward(step, drive, in_wide, out_wide, rate, entry):
    t = Tiling(*step.shape, False)
    per = t.per

    def kernel(*refs):
        step_refs, drive_refs = refs[:per], refs[per : 2 * per]
        in_ref, out_ref, rate_ref, entry_ref, y_ref, before_ref, last_ref = refs[2 * per :]

        @pl.when(pl.program_id(1) == 0)
        def _():
            last_ref[...] = entry_ref[...]

        rates = t.load(rate_ref)

        def some(i, state):
            state = list(state)
            base = pl.multiple_of(i * ROWS, ROWS)
            sums = [[None] * ROWS for _ in range(per)]
            for j in range(ROWS):
                token = base + j
                ins, outs = pair(in_ref, token), pair(out_ref, token)
                for g in range(per):
                    now = spread(step_refs[g], token)
                    force = spread(drive_refs[g], token)
                    total = None
                    for k in (0, 1):
                        m = 2 * g + k
                        before_ref[token, 8 * k : 8 * k + 8, t.lanes[g]] = state[m]
                        state[m] = jnp.exp2(now * rates[m]) * state[m] + force * ins[k]
                        term = state[m] * outs[k]
                        total = term if total is None else total + term
                    sums[g][j] = total
            for g in range(per):
                y_ref[pl.ds(base, ROWS), t.lanes[g]] = fold_rows(sums[g])
            return tuple(state)

        t.store(last_ref, lax.fori_loop(0, t.block // ROWS, some, t.load(last_ref)))

    return t.call(
        kernel,
        "scan_forward",
        t.narrow()
        + t.narrow()
        + [t.wide_spec(), t.wide_spec(), t.state_spec(), t.state_spec()],
        (t.token_spec(), t.history_spec(), t.state_spec()),
        (
            f32(t.tokens, t.channels),
            f32(t.tokens, STATE, t.channels),
            f32(STATE, t.channels),
        ),
    )(*[step] * per, *[drive] * per, in_wide, out_wide, rate, entry)


def scan_backward(step, drive, back, in_wide, out_wide, rate, entry, before, last):
    t = Tiling(*step.shape, True)
    per = t.per

    def kernel(*refs):
        step_refs, drive_refs, back_refs = (refs[i * per : (i + 1) * per] for i in range(3))
        in_ref, out_ref, rate_ref, entry_ref, before_ref, last_ref = refs[
            3 * per : 3 * per + 6
        ]
        rate_sum_ref, in_sum_ref, decay_ref, in_part_ref, out_part_ref = refs[
            3 * per + 6 : 3 * per + 11
        ]
        carry_ref, state_ref = refs[3 * per + 11 :]

        @pl.when(pl.program_id(1) == 0)
        def _():
            decay_ref[...] = jnp.zeros_like(decay_ref)
            carry_ref[...] = entry_ref[...]
            state_ref[...] = last_ref[...]

        rates = t.load(rate_ref)

        def some(i, carried):
            carry, state, decay = (list(part) for part in carried)
            base = pl.multiple_of(t.block - ROWS - i * ROWS, ROWS)
            rate_sums = [[None] * ROWS for _ in range(per)]
            in_sums = [[None] * ROWS for _ in range(per)]
            for j in range(ROWS - 1, -1, -1):
                token = base + j
                ins, outs = pair(in_ref, token), pair(out_ref, token)
                in_part, out_part = [None, None], [None, None]
                for g in range(per):
                    now = spread(step_refs[g], token)
                    force = spread(drive_refs[g], token)
                    above = spread(back_refs[g], token)
                    by_rate, by_in = [None, None], [None, None]
                    for k in (0, 1):
                        m = 2 * g + k
                        earlier = before_ref[token, 8 * k : 8 * k + 8, t.lanes[g]]
                        grad = carry[m] + above * outs[k]
                        carry[m] = jnp.exp2(now * rates[m]) * grad
                        weighted = carry[m] * earlier
                        decay[m] = decay[m] + weighted * now
                        by_rate[k] = weighted * rates[m]
                        by_in[k] = grad * ins[k]
                        for parts, term in (
                            (in_part, grad * force),
                            (out_part, above * state[m]),
                        ):
                            parts[k] = term if parts[k] is None else parts[k] + term
                        state[m] = earlier
                    rate_sums[g][j] = by_rate[0] + by_rate[1]
                    in_sums[g][j] = by_in[0] + by_in[1]
                for k in (0, 1):
                    in_part_ref[0, token, 8 * k : 8 * k + 8, :] = in_part[k]
                    out_part_ref[0, token, 8 * k : 8 * k + 8, :] = out_part[k]
            for g in range(per):
                rate_sum_ref[pl.ds(base, ROWS), t.lanes[g]] = fold_rows(rate_sums[g])
                in_sum_ref[pl.ds(base, ROWS), t.lanes[g]] = fold_rows(in_sums[g])
            return tuple(carry), tuple(state), tuple(decay)

        carry, state, decay = lax.fori_loop(
            0,
            t.block // ROWS,
            some,
            (t.load(carry_ref), t.load(state_ref), t.load(decay_ref)),
        )
        t.store(carry_ref, carry)
        t.store(state_ref, state)
        t.store(decay_ref, decay)

    parts = f32(t.grid[0], t.tokens, STATE, LANES)
    rate_sum, in_sum, decay, in_part, out_part = t.call(
        kernel,
        "scan_backward",
        t.narrow()
        + t.narrow()
        + t.narrow()
        + [
            t.wide_spec(),
            t.wide_spec(),
            t.state_spec(),
            t.state_spec(),
            t.history_spec(),
            t.state_spec(),
        ],
        (t.token_spec(), t.token_spec(), t.state_spec(), t.part_spec(), t.part_spec()),
        (
            f32(t.tokens, t.channels),
            f32(t.tokens, t.channels),
            f32(STATE, t.channels),
            parts,
            parts,
        ),
        [pltpu.VMEM((STATE, t.width), jnp.float32)] * 2,
    )(
        *[step] * per,
        *[drive] * per,
        *[back] * per,
        in_wide,
        out_wide,
        rate,
        entry,
        before,
        last,
    )
    return rate_sum, in_sum, decay, jnp.sum(in_part, (0, 3)), jnp.sum(out_part, (0, 3))


def chunk_entry(state, step_total, rate, direction):
    packed = jnp.concatenate([state, step_total], axis=0)
    entry = None
    for distance in range(lax.axis_size("col") - 1, 0, -1):
        got = shift(packed, "col", direction * distance)
        if entry is None:
            entry = got[:STATE]
        else:
            entry = got[:STATE] + jnp.exp2(got[STATE:] * rate) * entry
    return entry


def widen(coefficients):
    return jnp.broadcast_to(coefficients[:, :, None], coefficients.shape + (LANES,))


def norm_forward(values, weights):
    inverse = lax.rsqrt(jnp.mean(values * values, axis=1, keepdims=True) + epsilon)
    scaled = values * inverse
    return scaled, inverse, low(scaled * weights)


def norm_backward(upstream, scaled, inverse, weights):
    weighted = upstream * weights
    inner_mean = jnp.mean(weighted * scaled, axis=1, keepdims=True)
    return (
        inverse * (weighted - scaled * inner_mean),
        jnp.sum(upstream * scaled, axis=0, keepdims=True),
    )


def body(
    tokens,
    mixer_norm,
    in_value,
    in_gate,
    conv_weight,
    conv_bias,
    state_proj,
    step_proj,
    step_bias,
    decay_log,
    skip_gain,
    mixer_out,
    feed_norm,
    feed_gate,
    feed_up,
    feed_down,
    out_grad,
):
    channels, units = in_value.shape[1], feed_gate.shape[1]
    in_low = gather_weight(jnp.concatenate([in_value, in_gate], axis=1), 0)
    mixer_low = gather_weight(mixer_out, 1)
    feed_low = gather_weight(jnp.concatenate([feed_gate, feed_up], axis=1), 0)
    feed_down_low = gather_weight(feed_down, 1)

    inputs = to_whole_features(tokens).astype(jnp.float32)
    out_back_low = to_whole_features(out_grad)
    gains = gather_by_swaps(jnp.stack([mixer_norm, feed_norm]), "col", 1)
    mixer_gain, feed_gain = gains[0:1], gains[1:2]
    packed = jnp.concatenate(
        [
            conv_weight.T,
            conv_bias[None],
            step_bias[None],
            skip_gain[None],
            decay_log.T,
        ],
        axis=0,
    )
    packed = gather_by_swaps(packed, "col", 1)
    taps = packed[:CONV]
    conv_bias_row, step_bias_row, skip_row = (
        packed[CONV + i : CONV + i + 1] for i in range(3)
    )
    decay_rate = -jnp.exp(packed[CONV + 3 :])
    state_low = gather_by_swaps(low(state_proj), "col", 0)
    step_weight = gather_by_swaps(low(step_proj), "col", 1)

    scaled_first, inverse_first, normed_first = norm_forward(inputs, mixer_gain)
    normed_all = row_gather(normed_first)
    grad_all = row_gather(out_back_low)
    both_in = product(normed_all, in_low)
    mixer_in, gate_in = both_in[:, :channels], both_in[:, channels:]
    count = mixer_in.shape[0]
    earlier = shift(mixer_in[-ROWS:], "col", 1)
    padded = jnp.concatenate([earlier[ROWS - CONV + 1 :], mixer_in], axis=0)
    conv_out = conv_bias_row + sum(
        padded[k : k + count] * taps[k : k + 1] for k in range(CONV)
    )
    conv_act = low(sigmoid_linear(conv_out))
    projected = row_total(product(conv_act, state_low))
    step_low = low(projected[:, :DT_RANK])
    in_wide = widen(projected[:, DT_RANK : DT_RANK + STATE])
    out_wide = widen(projected[:, DT_RANK + STATE :])
    step_pre = product(step_low, step_weight) + step_bias_row
    step_size = jax.nn.softplus(step_pre)
    act_float = conv_act.astype(jnp.float32)
    drive = step_size * act_float
    rate = decay_rate * LOG2E
    step_total = jnp.sum(step_size, axis=0, keepdims=True)
    handed = chunk_state(step_size, drive, in_wide, rate, False)
    entry = chunk_entry(handed, step_total, rate, 1)
    scanned, before, last = scan_forward(step_size, drive, in_wide, out_wide, rate, entry)
    scan_out = scanned + skip_row * act_float
    gate_act = sigmoid_linear(gate_in)
    gated = low(scan_out * gate_act)
    middle = inputs + row_scatter(product(gated, mixer_low))

    scaled_second, inverse_second, normed_second = norm_forward(middle, feed_gain)
    normed_feed = row_gather(normed_second)
    both_pre = product(normed_feed, feed_low)
    gate_pre, up_pre = both_pre[:, :units], both_pre[:, units:]
    gate_swish = sigmoid_linear(gate_pre)
    hidden = low(gate_swish * up_pre)
    feed_down_grad = low(product(hidden, grad_all, contract_first))
    hidden, feed_down_grad = lax.optimization_barrier((hidden, feed_down_grad))
    down_own = scatter_gradient(feed_down_grad, 1)
    output = to_feature_blocks(low(middle + row_scatter(product(hidden, feed_down_low))))

    hidden_back = product(grad_all, feed_down_low, contract_last)
    gate_back = low(hidden_back * up_pre * sigmoid_slope(gate_pre))
    up_back = low(hidden_back * gate_swish)
    both_back = jnp.concatenate([gate_back, up_back], axis=1)
    feed_grad = low(product(normed_feed, both_back, contract_first))
    both_back, feed_grad = lax.optimization_barrier((both_back, feed_grad))
    feed_own = scatter_gradient(feed_grad, 0)
    normed_back = row_scatter(product(both_back, feed_low, contract_last))
    middle_norm, feed_norm_part = norm_backward(
        normed_back, scaled_second, inverse_second, feed_gain
    )
    middle_back = out_back_low.astype(jnp.float32) + middle_norm
    middle_all = row_gather(low(middle_back))

    mixer_out_grad = low(product(gated, middle_all, contract_first))
    middle_all, mixer_out_grad = lax.optimization_barrier((middle_all, mixer_out_grad))
    mixer_own = scatter_gradient(mixer_out_grad, 1)
    mixer_out_grad = both_halves(mixer_own, 1)
    gated_back = product(middle_all, mixer_low, contract_last)
    scan_back = gated_back * gate_act
    gate_in_back = low(gated_back * scan_out * sigmoid_slope(gate_in))
    in_gate_grad = low(product(normed_all, gate_in_back, contract_first))
    scan_back, in_gate_grad = lax.optimization_barrier((scan_back, in_gate_grad))
    gate_own = scatter_gradient(in_gate_grad, 0)
    in_gate_grad = both_halves(gate_own, 0)
    handed_back = chunk_state(step_size, scan_back, out_wide, rate, True)
    entry_back = chunk_entry(handed_back, step_total, rate, -1)
    rate_sum, in_sum, decay_sum, in_back, out_back = scan_backward(
        step_size, drive, scan_back, in_wide, out_wide, rate, entry_back, before, last
    )
    step_back = rate_sum * LN2 + act_float * in_sum
    act_scan = step_size * in_sum + skip_row * scan_back
    pre_back = step_back * jax.nn.sigmoid(step_pre)
    pre_low = low(pre_back)
    rank_back = product(pre_low, step_weight, contract_last)
    proj_back = low(row_total(jnp.concatenate([rank_back, in_back, out_back], axis=1)))
    act_back = act_scan + product(proj_back, state_low, contract_last)
    conv_back = act_back * sigmoid_slope(conv_out)
    later = shift(conv_back[:ROWS], "col", -1)
    trailing = jnp.concatenate([conv_back, later[: CONV - 1]], axis=0)
    mixer_back = low(
        sum(
            trailing[CONV - 1 - k : CONV - 1 - k + count] * taps[k : k + 1]
            for k in range(CONV)
        )
    )
    in_value_grad = low(product(normed_all, mixer_back, contract_first))
    mixer_back, in_value_grad, down_own, feed_own = lax.optimization_barrier(
        (mixer_back, in_value_grad, down_own, feed_own)
    )
    feed_down_grad = both_halves(down_own, 1)
    feed_grad = both_halves(feed_own, 0)
    in_value_grad = both_halves(scatter_gradient(in_value_grad, 0), 0)
    both_in_back = jnp.concatenate([mixer_back, gate_in_back], axis=1)
    normed_first_back = row_scatter(product(both_in_back, in_low, contract_last))
    input_norm, mixer_norm_part = norm_backward(
        normed_first_back, scaled_first, inverse_first, mixer_gain
    )
    tokens_grad = to_feature_blocks(low(middle_back + input_norm)).astype(jnp.float32)

    def over_tokens(values):
        return jnp.sum(values, axis=0, keepdims=True)

    packed_grad = jnp.concatenate(
        [over_tokens(conv_back * padded[k : k + count]) for k in range(CONV)]
        + [
            over_tokens(conv_back),
            over_tokens(pre_back),
            over_tokens(scan_back * act_float),
            decay_sum * decay_rate,
        ],
        axis=0,
    )

    def over_group(values, axis, dtype):
        own = scatter_by_swaps(values, "col", axis, dtype)
        return own + swap(own, "dp", 1)

    packed_grad = over_group(packed_grad, 1, jnp.float32)
    state_proj_grad = over_group(
        product(conv_act, proj_back, contract_first), 0, jnp.bfloat16
    )
    step_proj_grad = over_group(product(step_low, pre_low, contract_first), 1, jnp.bfloat16)
    gain_sums = scatter_by_swaps(
        jnp.concatenate([mixer_norm_part, feed_norm_part], axis=0), "col", 1, jnp.float32
    )
    gain_sums = lax.psum(gain_sums, ("dp", "row"))
    return (
        output,
        tokens_grad,
        gain_sums[0],
        in_value_grad,
        in_gate_grad,
        packed_grad[:CONV].T,
        packed_grad[CONV],
        state_proj_grad,
        step_proj_grad,
        packed_grad[CONV + 1],
        packed_grad[CONV + 3 :].T,
        packed_grad[CONV + 2],
        mixer_out_grad,
        gain_sums[1],
        feed_grad[:, :units],
        feed_grad[:, units:],
        feed_down_grad,
    )


def solution(mesh):
    token_spec = P(("dp", "row"), "col")
    weight_in, weight_out = P("col", "row"), P("row", "col")
    channel, channel_rows = P(("row", "col")), P(("row", "col"), None)
    parameters = (
        P("col"),
        weight_in,
        weight_in,
        channel_rows,
        channel,
        channel_rows,
        P(None, ("row", "col")),
        channel,
        channel_rows,
        channel,
        weight_out,
        P("col"),
        weight_in,
        weight_in,
        weight_out,
    )
    return jax.shard_map(
        body,
        mesh=mesh,
        in_specs=(token_spec,) + parameters + (token_spec,),
        out_specs=(token_spec, token_spec) + parameters,
        check_vma=False,
    )
```

```python
import jax
import jax.numpy as jnp
import numpy as np
from jax import lax
from jax.experimental import pallas as pl
from jax.experimental.pallas import tpu as pltpu
from jax.sharding import PartitionSpec as P

STATE = 16
CONV = 4
DT_RANK = 128
LANES = 128
ROWS = 8
LOG2E = np.float32(np.log2(np.e))
LN2 = np.float32(np.log(2.0))

epsilon = 1e-05
contract_first = (((0,), (0,)), ((), ()))
contract_last = (((1,), (1,)), ((), ()))
contract_inner = (((1,), (0,)), ((), ()))


def sigmoid_linear(values):
    return values * jax.nn.sigmoid(values)


def sigmoid_slope(values):
    logistic = jax.nn.sigmoid(values)
    return logistic * (1.0 + values * (1.0 - logistic))


def product(multiplicand, multiplier, dims=contract_inner):
    return lax.dot_general(multiplicand, multiplier, dims, preferred_element_type=jnp.float32)


def low(values):
    return values.astype(jnp.bfloat16)


def swap(values, axis, distance):
    return lax.ppermute(
        values, axis, [(i, i ^ distance) for i in range(lax.axis_size(axis))]
    )


def shift(values, axis, distance):
    size = lax.axis_size(axis)
    pairs = [(i, i + distance) for i in range(size) if 0 <= i + distance < size]
    return lax.ppermute(values, axis, pairs)


def gather_by_swaps(values, axis_name, axis):
    size, length = lax.axis_size(axis_name), values.shape[axis]
    index = lax.axis_index(axis_name)
    shape = list(values.shape)
    shape[axis] = size * length
    joined = jnp.zeros(shape, values.dtype)
    for distance in range(size):
        part = swap(values, axis_name, distance) if distance else values
        joined = lax.dynamic_update_slice_in_dim(
            joined, part, (index ^ distance) * length, axis
        )
    return joined


def gather_blocks(values):
    return gather_by_swaps(values[None], "col", 0)


def scatter_by_swaps(values, axis_name, axis, dtype):
    size = lax.axis_size(axis_name)
    length = values.shape[axis] // size
    index = lax.axis_index(axis_name)

    def block(distance):
        return lax.dynamic_slice_in_dim(values, (index ^ distance) * length, length, axis)

    total = block(0).astype(jnp.float32)
    for distance in range(1, size):
        total = total + swap(block(distance).astype(dtype), axis_name, distance).astype(
            jnp.float32
        )
    return total


def by_swaps():
    return lax.axis_size("row") == 4


def block_order():
    return lax.axis_index("row") if by_swaps() else jnp.int32(0)


def row_gather(values):
    if by_swaps():
        return jnp.concatenate(
            [values] + [swap(values, "row", distance) for distance in range(1, 4)], axis=0
        )
    return lax.all_gather(values, "row", axis=0, tiled=True)


def row_scatter(values):
    if by_swaps():
        count = values.shape[0] // 4
        total = values[:count]
        for distance in range(1, 4):
            block = low(values[distance * count : (distance + 1) * count])
            total = total + swap(block, "row", distance).astype(jnp.float32)
        return total
    return lax.psum_scatter(low(values), "row", scatter_dimension=0, tiled=True).astype(
        jnp.float32
    )


def row_total(values, local=None):
    if by_swaps():
        blocks = values.reshape((4, -1) + values.shape[1:])
        total = (values if local is None else local).reshape(blocks.shape)
        for distance in range(1, 4):
            got = swap(values, "row", distance).reshape(blocks.shape)
            total = total + jnp.concatenate(
                [got[k ^ distance : (k ^ distance) + 1] for k in range(4)], axis=0
            )
        return total.reshape(values.shape)
    return lax.psum(values, "row")


def block_moves():
    rows, cols = lax.axis_size("row"), lax.axis_size("col")
    return [(k, (k % rows) * cols + k // rows) for k in range(rows * cols)]


def exchange(pieces, axis_name):
    index = lax.axis_index(axis_name)
    joined = jnp.zeros_like(pieces)
    for distance in range(lax.axis_size(axis_name)):
        part = lax.dynamic_slice_in_dim(pieces, index ^ distance, 1, 0)
        if distance:
            part = swap(part, axis_name, distance)
        joined = lax.dynamic_update_slice_in_dim(joined, part, index ^ distance, 0)
    return joined


def to_whole_features(values):
    rows, cols = lax.axis_size("row"), lax.axis_size("col")
    if rows == cols:
        count, features = values.shape
        pieces = values.reshape(rows, count // rows, features)
        pieces = exchange(exchange(pieces, "row"), "col")
        return jnp.concatenate([pieces[c] for c in range(cols)], axis=1)
    split = lax.all_to_all(values, "col", split_axis=0, concat_axis=1, tiled=True)
    return lax.ppermute(split, ("row", "col"), block_moves())


def to_feature_blocks(arrays, others):
    rows, cols = lax.axis_size("row"), lax.axis_size("col")
    count, features = arrays[0].shape[0], arrays[0].shape[1] // cols
    if rows == cols:
        pieces = jnp.stack(
            [
                jnp.concatenate(
                    [values[:, c * features : (c + 1) * features] for values in arrays]
                )
                for c in range(cols)
            ]
        )
        pieces = lax.all_to_all(pieces, "col", split_axis=0, concat_axis=0)
        pieces, others = lax.optimization_barrier((pieces, others))
        pieces = exchange(pieces, "row")
        return [
            pieces[:, i * count : (i + 1) * count].reshape(rows * count, features)
            for i in range(len(arrays))
        ], others
    back = [(target, source) for source, target in block_moves()]

    def one(values):
        split = lax.ppermute(values, ("row", "col"), back)
        return lax.all_to_all(split, "col", split_axis=1, concat_axis=0, tiled=True)

    return [one(values) for values in arrays], others


def gather_weight(weight):
    half = weight.shape[0] // lax.axis_size("dp")
    part = lax.dynamic_slice_in_dim(weight, lax.axis_index("dp") * half, half, 0)
    return lax.all_gather(low(part), ("col", "dp"), axis=0, tiled=True)


def block_at(blocks, place):
    return lax.dynamic_index_in_dim(blocks, place, 0, keepdims=False)


def neighbours(outside, blocks, order, direction):
    last = blocks.shape[0] - 1
    edge = 0 if direction == -1 else last
    got = []
    for place in range(last + 1):
        own = place ^ order
        near = block_at(blocks, jnp.clip(own + direction, 0, last) ^ order)
        got.append(jnp.where(own == edge, outside, near))
    return jnp.stack(got)


def feature_halves(values):
    blocks, first = lax.axis_size("col"), lax.axis_index("dp") == 0
    half = values.shape[1] // (2 * blocks)
    parts = [values[:, i * half : (i + 1) * half] for i in range(2 * blocks)]
    upper, lower = jnp.concatenate(parts[0::2], axis=1), jnp.concatenate(parts[1::2], axis=1)
    return jnp.where(first, upper, lower), jnp.where(first, lower, upper)


def add_pair(own, other):
    return low(own + swap(other, "dp", 1).astype(jnp.float32))


def scatter_gradient(gradient):
    return lax.psum_scatter(gradient, "col", scatter_dimension=0, tiled=True)


def both_halves(own, axis):
    other = swap(own, "dp", 1)
    first = lax.axis_index("dp") == 0
    return jnp.concatenate(
        [jnp.where(first, own, other), jnp.where(first, other, own)], axis=axis
    )


def fold_rows(parts):
    row = lax.broadcasted_iota(jnp.int32, parts[0].shape, 0)
    for half in (1, 2, 4):
        mask = (row & half) == 0
        parts = [
            jnp.where(mask, a, b) + pltpu.roll(jnp.where(mask, b, a), ROWS - half, 0)
            for a, b in zip(parts[0::2], parts[1::2])
        ]
    return parts[0]


def spread(ref, token):
    return ref[pl.ds(token, ROWS, stride=0), :]


class Tiling:
    def __init__(self, order, tokens, channels, backward):
        self.order = order
        groups = channels // LANES
        self.tokens, self.channels = tokens, channels
        self.per = min(8, groups)
        self.block = min(tokens // lax.axis_size("row") if by_swaps() else 128, tokens)
        self.blocks = tokens // self.block
        self.grid = (groups // self.per, self.blocks)
        self.width = self.per * LANES
        self.backward = backward
        self.lanes = [slice(g * LANES, (g + 1) * LANES) for g in range(self.per)]

    def at(self, b):
        return self.blocks - 1 - b if self.backward else b

    def narrow(self):
        def spec(i):
            return pl.BlockSpec(
                (self.block, LANES), lambda g, b, order: (self.at(b) ^ order[0], g * self.per + i)
            )

        return [spec(i) for i in range(self.per)]

    def token_spec(self):
        return pl.BlockSpec(
            (self.block, self.width), lambda g, b, order: (self.at(b) ^ order[0], g)
        )

    def wide_spec(self):
        return pl.BlockSpec(
            (self.block, STATE, LANES), lambda g, b, order: (self.at(b) ^ order[0], 0, 0)
        )

    def state_spec(self):
        return pl.BlockSpec((STATE, self.width), lambda g, b, order: (0, g))

    def history_spec(self):
        return pl.BlockSpec(
            (self.block, STATE, self.width), lambda g, b, order: (self.at(b), 0, g)
        )

    def part_spec(self):
        return pl.BlockSpec(
            (1, self.block, LANES), lambda g, b, order: (g, self.at(b) ^ order[0], 0)
        )

    def load(self, ref):
        out = []
        for lanes in self.lanes:
            out += [ref[0:8, lanes], ref[8:16, lanes]]
        return tuple(out)

    def store(self, ref, values):
        for g, lanes in enumerate(self.lanes):
            ref[0:8, lanes] = values[2 * g]
            ref[8:16, lanes] = values[2 * g + 1]

    def call(self, kernel, name, in_specs, out_specs, out_shape, scratch=()):
        call = pl.pallas_call(
            kernel,
            out_shape=out_shape,
            grid_spec=pltpu.PrefetchScalarGridSpec(
                num_scalar_prefetch=1,
                grid=self.grid,
                in_specs=in_specs,
                out_specs=out_specs,
                scratch_shapes=list(scratch),
            ),
            compiler_params=pltpu.CompilerParams(
                dimension_semantics=("arbitrary", "arbitrary"),
                vmem_limit_bytes=56 * 2**20,
            ),
            name=name,
        )
        return lambda *operands: call(self.order.reshape(1), *operands)


def pair(ref, token):
    return ref[token, 0:8, :], ref[token, 8:16, :]


def f32(*shape):
    return jax.ShapeDtypeStruct(shape, jnp.float32)


def chunk_state(order, step, drive, wide, rate, backward):
    t = Tiling(order, *step.shape, backward)
    per = t.per

    def kernel(_, *refs):
        step_refs, drive_refs = refs[:per], refs[per : 2 * per]
        wide_ref, rate_ref, state_ref = refs[2 * per :]

        @pl.when(pl.program_id(1) == 0)
        def _():
            state_ref[...] = jnp.zeros_like(state_ref)

        rates = t.load(rate_ref)

        def some(i, state):
            state = list(state)
            base = t.block - ROWS - i * ROWS if backward else i * ROWS
            for j in range(ROWS - 1, -1, -1) if backward else range(ROWS):
                token = base + j
                wides = pair(wide_ref, token)
                for g in range(per):
                    now = spread(step_refs[g], token)
                    force = spread(drive_refs[g], token)
                    for k in (0, 1):
                        m = 2 * g + k
                        factor = jnp.exp2(now * rates[m])
                        if backward:
                            state[m] = factor * (state[m] + force * wides[k])
                        else:
                            state[m] = factor * state[m] + force * wides[k]
            return tuple(state)

        t.store(
            state_ref, lax.fori_loop(0, t.block // ROWS, some, t.load(state_ref))
        )

    return t.call(
        kernel,
        "chunk_state_back" if backward else "chunk_state",
        t.narrow() + t.narrow() + [t.wide_spec(), t.state_spec()],
        t.state_spec(),
        f32(STATE, t.channels),
    )(*[step] * per, *[drive] * per, wide, rate)


def scan_forward(order, step, drive, in_wide, out_wide, rate, entry):
    t = Tiling(order, *step.shape, False)
    per = t.per

    def kernel(_, *refs):
        step_refs, drive_refs = refs[:per], refs[per : 2 * per]
        in_ref, out_ref, rate_ref, entry_ref, y_ref, before_ref, last_ref = refs[2 * per :]

        @pl.when(pl.program_id(1) == 0)
        def _():
            last_ref[...] = entry_ref[...]

        rates = t.load(rate_ref)

        def some(i, state):
            state = list(state)
            base = pl.multiple_of(i * ROWS, ROWS)
            sums = [[None] * ROWS for _ in range(per)]
            for j in range(ROWS):
                token = base + j
                ins, outs = pair(in_ref, token), pair(out_ref, token)
                for g in range(per):
                    now = spread(step_refs[g], token)
                    force = spread(drive_refs[g], token)
                    total = None
                    for k in (0, 1):
                        m = 2 * g + k
                        before_ref[token, 8 * k : 8 * k + 8, t.lanes[g]] = state[m]
                        state[m] = jnp.exp2(now * rates[m]) * state[m] + force * ins[k]
                        term = state[m] * outs[k]
                        total = term if total is None else total + term
                    sums[g][j] = total
            for g in range(per):
                y_ref[pl.ds(base, ROWS), t.lanes[g]] = fold_rows(sums[g])
            return tuple(state)

        t.store(last_ref, lax.fori_loop(0, t.block // ROWS, some, t.load(last_ref)))

    return t.call(
        kernel,
        "scan_forward",
        t.narrow()
        + t.narrow()
        + [t.wide_spec(), t.wide_spec(), t.state_spec(), t.state_spec()],
        (t.token_spec(), t.history_spec(), t.state_spec()),
        (
            f32(t.tokens, t.channels),
            f32(t.tokens, STATE, t.channels),
            f32(STATE, t.channels),
        ),
    )(*[step] * per, *[drive] * per, in_wide, out_wide, rate, entry)


def scan_backward(order, step, drive, back, in_wide, out_wide, rate, entry, before, last):
    t = Tiling(order, *step.shape, True)
    per = t.per

    def kernel(_, *refs):
        step_refs, drive_refs, back_refs = (refs[i * per : (i + 1) * per] for i in range(3))
        in_ref, out_ref, rate_ref, entry_ref, before_ref, last_ref = refs[
            3 * per : 3 * per + 6
        ]
        rate_sum_ref, in_sum_ref, decay_ref, coefficient_ref = refs[3 * per + 6 : 3 * per + 10]
        carry_ref, state_ref, in_part_ref, out_part_ref = refs[3 * per + 10 :]

        @pl.when(pl.program_id(1) == 0)
        def _():
            decay_ref[...] = jnp.zeros_like(decay_ref)
            carry_ref[...] = entry_ref[...]
            state_ref[...] = last_ref[...]

        rates = t.load(rate_ref)

        def some(i, carried):
            carry, state, decay = (list(part) for part in carried)
            base = pl.multiple_of(t.block - ROWS - i * ROWS, ROWS)
            rate_sums = [[None] * ROWS for _ in range(per)]
            in_sums = [[None] * ROWS for _ in range(per)]
            for j in range(ROWS - 1, -1, -1):
                token = base + j
                ins, outs = pair(in_ref, token), pair(out_ref, token)
                in_part, out_part = [None, None], [None, None]
                for g in range(per):
                    now = spread(step_refs[g], token)
                    force = spread(drive_refs[g], token)
                    above = spread(back_refs[g], token)
                    by_rate, by_in = [None, None], [None, None]
                    for k in (0, 1):
                        m = 2 * g + k
                        earlier = before_ref[token, 8 * k : 8 * k + 8, t.lanes[g]]
                        grad = carry[m] + above * outs[k]
                        carry[m] = jnp.exp2(now * rates[m]) * grad
                        weighted = carry[m] * earlier
                        decay[m] = decay[m] + weighted * now
                        by_rate[k] = weighted * rates[m]
                        by_in[k] = grad * ins[k]
                        for parts, term in (
                            (in_part, grad * force),
                            (out_part, above * state[m]),
                        ):
                            parts[k] = term if parts[k] is None else parts[k] + term
                        state[m] = earlier
                    rate_sums[g][j] = by_rate[0] + by_rate[1]
                    in_sums[g][j] = by_in[0] + by_in[1]
                for k in (0, 1):
                    place = pl.multiple_of(token * STATE + k * ROWS, ROWS)
                    in_part_ref[pl.ds(place, ROWS), :] = in_part[k]
                    out_part_ref[pl.ds(place, ROWS), :] = out_part[k]
            for g in range(per):
                rate_sum_ref[pl.ds(base, ROWS), t.lanes[g]] = fold_rows(rate_sums[g])
                in_sum_ref[pl.ds(base, ROWS), t.lanes[g]] = fold_rows(in_sums[g])
            return tuple(carry), tuple(state), tuple(decay)

        carry, state, decay = lax.fori_loop(
            0,
            t.block // ROWS,
            some,
            (t.load(carry_ref), t.load(state_ref), t.load(decay_ref)),
        )
        t.store(carry_ref, carry)
        t.store(state_ref, state)
        t.store(decay_ref, decay)

        for part_ref in (in_part_ref, out_part_ref):
            part = part_ref[...]
            high = low(part)
            ones = jnp.ones((LANES, LANES), jnp.bfloat16)
            part_ref[...] = product(high, ones) + product(
                low(part - high.astype(jnp.float32)), ones
            )
        row = lax.broadcasted_iota(jnp.int32, (ROWS, LANES), 0)
        lane = lax.broadcasted_iota(jnp.int32, (ROWS, LANES), 1)

        def gathered(i, _):
            base = pl.multiple_of(i * ROWS, ROWS)
            tokens = []
            for j in range(ROWS):
                total = None
                for m, part_ref in ((0, in_part_ref), (1, out_part_ref)):
                    for k in (0, 1):
                        place = pl.multiple_of((base + j) * STATE + k * ROWS, ROWS)
                        term = jnp.where(
                            lane == row + (m * STATE + k * ROWS),
                            part_ref[pl.ds(place, ROWS), :],
                            0.0,
                        )
                        total = term if total is None else total + term
                tokens.append(total)
            coefficient_ref[0, pl.ds(base, ROWS), :] = fold_rows(tokens)
            return _

        lax.fori_loop(0, t.block // ROWS, gathered, 0)

    rate_sum, in_sum, decay, coefficients = t.call(
        kernel,
        "scan_backward",
        t.narrow()
        + t.narrow()
        + t.narrow()
        + [
            t.wide_spec(),
            t.wide_spec(),
            t.state_spec(),
            t.state_spec(),
            t.history_spec(),
            t.state_spec(),
        ],
        (t.token_spec(), t.token_spec(), t.state_spec(), t.part_spec()),
        (
            f32(t.tokens, t.channels),
            f32(t.tokens, t.channels),
            f32(STATE, t.channels),
            f32(t.grid[0], t.tokens, LANES),
        ),
        [pltpu.VMEM((STATE, t.width), jnp.float32)] * 2
        + [pltpu.VMEM((t.block * STATE, LANES), jnp.float32)] * 2,
    )(
        *[step] * per,
        *[drive] * per,
        *[back] * per,
        in_wide,
        out_wide,
        rate,
        entry,
        before,
        last,
    )
    return rate_sum, in_sum, decay, jnp.sum(coefficients, 0)[:, : 2 * STATE]


def chunk_entry(state, step_total, rate, direction):
    packed = jnp.concatenate([state, step_total], axis=0)
    entry = None
    for distance in range(lax.axis_size("col") - 1, 0, -1):
        got = shift(packed, "col", direction * distance)
        if entry is None:
            entry = got[:STATE]
        else:
            entry = got[:STATE] + jnp.exp2(got[STATE:] * rate) * entry
    return entry


def widen(coefficients):
    return jnp.broadcast_to(coefficients[:, :, None], coefficients.shape + (LANES,))


def norm_forward(values, weights):
    inverse = lax.rsqrt(jnp.mean(values * values, axis=1, keepdims=True) + epsilon)
    scaled = values * inverse
    return scaled, inverse, low(scaled * weights)


def norm_backward(upstream, scaled, inverse, weights):
    weighted = upstream * weights
    inner_mean = jnp.mean(weighted * scaled, axis=1, keepdims=True)
    return (
        inverse * (weighted - scaled * inner_mean),
        jnp.sum(upstream * scaled, axis=0, keepdims=True),
    )


def body(
    tokens,
    mixer_norm,
    in_value,
    in_gate,
    conv_weight,
    conv_bias,
    state_proj,
    step_proj,
    step_bias,
    decay_log,
    skip_gain,
    mixer_out,
    feed_norm,
    feed_gate,
    feed_up,
    feed_down,
    out_grad,
):
    channels, units = in_value.shape[1], feed_gate.shape[1]
    order = block_order()
    rows, index = lax.axis_size("row"), lax.axis_index("dp")
    first = gather_weight(jnp.concatenate([in_value, in_gate, mixer_out.T], axis=1))
    in_low, mixer_low = first[:, : 2 * channels], first[:, 2 * channels :]
    feed_low = gather_weight(jnp.concatenate([feed_gate, feed_up], axis=1))
    feed_down_low = gather_weight(feed_down.T)

    inputs = to_whole_features(tokens)
    own_channels = conv_bias.shape[0]
    gains = jnp.stack([mixer_norm, feed_norm]).reshape(-1, own_channels)
    packed = jnp.concatenate(
        [
            gains,
            conv_weight.T,
            conv_bias[None],
            step_bias[None],
            skip_gain[None],
            decay_log.T,
        ],
        axis=0,
    )
    packed = gather_blocks(packed)
    gain_rows = gains.shape[0]
    gains = packed[:, :gain_rows].reshape(-1, 2, mixer_norm.shape[0])
    mixer_gain = gains[:, 0].reshape(1, -1)
    feed_gain = gains[:, 1].reshape(1, -1)
    packed = jnp.swapaxes(packed[:, gain_rows:], 0, 1).reshape(-1, channels)
    taps = packed[:CONV]
    conv_bias_row, step_bias_row, skip_row = (
        packed[CONV + i : CONV + i + 1] for i in range(3)
    )
    decay_rate = -jnp.exp(packed[CONV + 3 :])
    projections = jnp.concatenate([low(step_proj), low(state_proj).T], axis=0)
    projections, inputs = lax.optimization_barrier((projections, inputs))
    half = projections.shape[0] // 2
    projections = gather_blocks(
        lax.dynamic_slice_in_dim(projections, index * half, half, 0)
    )
    projections = both_halves(projections, 1)
    projections = jnp.swapaxes(projections, 0, 1).reshape(-1, channels)
    step_weight, state_low = projections[:DT_RANK], projections[DT_RANK:]
    inputs = inputs.astype(jnp.float32)

    scaled_first, inverse_first, normed_first = norm_forward(inputs, mixer_gain)
    normed_all = row_gather(normed_first)
    count = normed_all.shape[0]
    both_in = product(normed_all, in_low)
    both_in, out_grad = lax.optimization_barrier((both_in, out_grad))
    out_back_low = to_whole_features(out_grad)
    grad_all = row_gather(out_back_low)
    mixer_in, gate_in = both_in[:, :channels], both_in[:, channels:]
    mixer_in = mixer_in.reshape(rows, -1, channels)
    length = mixer_in.shape[1]
    tails = mixer_in[:, -ROWS:]
    outside = shift(block_at(tails, (rows - 1) ^ order), "col", 1)
    earlier = neighbours(outside, tails, order, -1)
    padded = jnp.concatenate([earlier[:, ROWS - CONV + 1 :], mixer_in], axis=1)
    conv_out = conv_bias_row + sum(
        padded[:, k : k + length] * taps[k : k + 1] for k in range(CONV)
    ).reshape(count, channels)
    conv_act = low(sigmoid_linear(conv_out))
    projected = row_total(product(conv_act, state_low, contract_last))
    step_low = low(projected[:, :DT_RANK])
    in_wide = widen(projected[:, DT_RANK : DT_RANK + STATE])
    out_wide = widen(projected[:, DT_RANK + STATE :])
    step_pre = product(step_low, step_weight) + step_bias_row
    step_size = jax.nn.softplus(step_pre)
    act_float = conv_act.astype(jnp.float32)
    drive = step_size * act_float
    rate = decay_rate * LOG2E
    step_total = jnp.sum(step_size, axis=0, keepdims=True)
    handed = chunk_state(order, step_size, drive, in_wide, rate, False)
    entry = chunk_entry(handed, step_total, rate, 1)
    scanned, before, last = scan_forward(
        order, step_size, drive, in_wide, out_wide, rate, entry
    )
    scan_out = scanned + skip_row * act_float
    gate_act = sigmoid_linear(gate_in)
    gated = low(scan_out * gate_act)
    middle = inputs + row_scatter(product(gated, mixer_low, contract_last))

    scaled_second, inverse_second, normed_second = norm_forward(middle, feed_gain)
    normed_feed = row_gather(normed_second)
    both_pre = product(normed_feed, feed_low)
    gate_pre, up_pre = both_pre[:, :units], both_pre[:, units:]
    gate_swish = sigmoid_linear(gate_pre)
    hidden = low(gate_swish * up_pre)
    grad_own, grad_other = feature_halves(grad_all)
    down_grad = add_pair(
        product(grad_own, hidden, contract_first),
        low(product(grad_other, hidden, contract_first)),
    )
    feed_down_low, down_grad = lax.optimization_barrier((feed_down_low, down_grad))
    down_own = scatter_gradient(down_grad)

    hidden_back = product(grad_all, feed_down_low)
    gate_back = low(hidden_back * up_pre * sigmoid_slope(gate_pre))
    up_back = low(hidden_back * gate_swish)
    both_back = jnp.concatenate([gate_back, up_back], axis=1)
    feed_left, feed_right = feature_halves(normed_feed)
    other_grad = low(product(feed_right, both_back, contract_first))
    both_back, other_grad = lax.optimization_barrier((both_back, other_grad))
    normed_back = product(both_back, feed_low, contract_last)
    feed_grad = add_pair(product(feed_left, both_back, contract_first), other_grad)
    normed_back, feed_grad = lax.optimization_barrier((normed_back, feed_grad))
    feed_own = scatter_gradient(feed_grad)
    normed_back = row_scatter(normed_back)
    middle_norm, feed_norm_part = norm_backward(
        normed_back, scaled_second, inverse_second, feed_gain
    )
    middle_back = out_back_low.astype(jnp.float32) + middle_norm
    middle_low, down_own = lax.optimization_barrier((low(middle_back), down_own))
    middle_all = row_gather(middle_low)

    gated_back = product(middle_all, mixer_low)
    scan_back = gated_back * gate_act
    gate_in_back = low(gated_back * scan_out * sigmoid_slope(gate_in))
    normed_own, normed_other = feature_halves(normed_all)
    middle_own, middle_other = feature_halves(middle_all)
    pair_own = jnp.concatenate(
        [
            product(middle_own, gated, contract_first),
            product(normed_own, gate_in_back, contract_first),
        ],
        axis=1,
    )
    pair_other = jnp.concatenate(
        [
            low(product(middle_other, gated, contract_first)),
            low(product(normed_other, gate_in_back, contract_first)),
        ],
        axis=1,
    )
    scan_back, hidden, pair_other = lax.optimization_barrier((scan_back, hidden, pair_other))
    pair_grad = add_pair(pair_own, pair_other)
    output = low(middle + row_scatter(product(hidden, feed_down_low, contract_last)))
    handed_back = chunk_state(order, step_size, scan_back, out_wide, rate, True)
    entry_back = chunk_entry(handed_back, step_total, rate, -1)
    rate_sum, in_sum, decay_sum, coefficient_back = scan_backward(
        order,
        step_size,
        drive,
        scan_back,
        in_wide,
        out_wide,
        rate,
        entry_back,
        before,
        last,
    )
    rate_sum, in_sum, coefficient_back, pair_grad, output = lax.optimization_barrier(
        (rate_sum, in_sum, coefficient_back, pair_grad, output)
    )
    step_back = rate_sum * LN2 + act_float * in_sum
    act_scan = step_size * in_sum + skip_row * scan_back
    pre_back = step_back * jax.nn.sigmoid(step_pre)
    pre_low = low(pre_back)
    rank_back = product(pre_low, step_weight, contract_last)
    partial = jnp.concatenate([rank_back, coefficient_back], axis=1)
    local, pair_grad, feed_own = lax.optimization_barrier((partial, pair_grad, feed_own))
    proj_back = low(row_total(partial, local))
    pair_own = scatter_gradient(pair_grad)
    act_back = act_scan + product(proj_back, state_low)
    conv_back = act_back * sigmoid_slope(conv_out)
    conv_blocks = conv_back.reshape(rows, length, channels)
    heads = conv_blocks[:, :ROWS]
    outside = shift(block_at(heads, order), "col", -1)
    later = neighbours(outside, heads, order, 1)
    trailing = jnp.concatenate([conv_blocks, later[:, : CONV - 1]], axis=1)
    mixer_back = low(
        sum(
            trailing[:, CONV - 1 - k : CONV - 1 - k + length] * taps[k : k + 1]
            for k in range(CONV)
        )
    ).reshape(count, channels)
    both_in_back = jnp.concatenate([mixer_back, gate_in_back], axis=1)
    normed_first_back = product(both_in_back, in_low, contract_last)
    mixer_back, normed_first_back = lax.optimization_barrier((mixer_back, normed_first_back))
    in_value_grad = add_pair(
        product(normed_own, mixer_back, contract_first),
        low(product(normed_other, mixer_back, contract_first)),
    )
    input_norm, mixer_norm_part = norm_backward(
        row_scatter(normed_first_back), scaled_first, inverse_first, mixer_gain
    )
    tokens_grad = low(middle_back + input_norm)

    def whole(own, after):
        own, _ = lax.optimization_barrier((own, after))
        return both_halves(own, 0)

    feed_grad = whole(feed_own, proj_back)
    down_grad = whole(down_own, proj_back)
    finished = (
        feed_grad[:, :units].astype(jnp.float32),
        feed_grad[:, units:].astype(jnp.float32),
        down_grad.T.astype(jnp.float32),
    )
    gain_parts = jnp.concatenate([mixer_norm_part, feed_norm_part], axis=0)
    in_value_grad, pair_own, tokens_grad, output, gain_parts, *finished = (
        lax.optimization_barrier(
            (in_value_grad, pair_own, tokens_grad, output, gain_parts) + finished
        )
    )
    feed_gate_out, feed_up_out, feed_down_out = finished
    value_own = scatter_gradient(in_value_grad)
    pair_grad = both_halves(pair_own, 0)
    finished = (
        pair_grad[:, channels:].astype(jnp.float32),
        pair_grad[:, :channels].T.astype(jnp.float32),
    )

    def over_tokens(values):
        return jnp.sum(values, axis=0, keepdims=True)

    gain_parts = gain_parts.reshape(2, lax.axis_size("col"), -1, own_channels)
    gain_parts = jnp.swapaxes(gain_parts, 1, 2).reshape(gain_rows, channels)
    packed_grad = jnp.concatenate(
        [gain_parts]
        + [
            jnp.sum(conv_blocks * padded[:, k : k + length], axis=(0, 1))[None]
            for k in range(CONV)
        ]
        + [
            over_tokens(conv_back),
            over_tokens(pre_back),
            over_tokens(scan_back * act_float),
            decay_sum * decay_rate,
        ],
        axis=0,
    )
    projection_grad = jnp.concatenate(
        [
            product(step_low, pre_low, contract_first),
            product(proj_back, conv_act, contract_first),
        ],
        axis=0,
    )
    (output, tokens_grad), (packed_grad, projection_grad) = to_feature_blocks(
        (output, tokens_grad), (packed_grad, projection_grad)
    )

    def over_group(values, dtype):
        own = scatter_by_swaps(values, "col", 1, dtype)
        return own + swap(own, "dp", 1)

    packed_grad = over_group(packed_grad, jnp.float32)
    half = projection_grad.shape[0] // 2
    mine, others = (
        lax.dynamic_slice_in_dim(projection_grad, place * half, half, 0)
        for place in (index, 1 - index)
    )
    mine = mine + swap(others, "dp", 1)
    projection_grad = both_halves(scatter_by_swaps(mine, "col", 1, jnp.bfloat16), 0)
    gain_sums = packed_grad[:gain_rows]
    distance = 1
    while distance < rows:
        gain_sums = gain_sums + swap(gain_sums, "row", distance)
        distance *= 2
    gain_sums = gain_sums.reshape(2, -1)
    packed_grad = packed_grad[gain_rows:]
    value_own, *finished = lax.optimization_barrier((value_own,) + finished)
    gate_out, mixer_out_grad = finished
    return (
        output,
        tokens_grad.astype(jnp.float32),
        gain_sums[0],
        both_halves(value_own, 0).astype(jnp.float32),
        gate_out,
        packed_grad[:CONV].T,
        packed_grad[CONV],
        projection_grad[DT_RANK:].T,
        projection_grad[:DT_RANK],
        packed_grad[CONV + 1],
        packed_grad[CONV + 3 :].T,
        packed_grad[CONV + 2],
        mixer_out_grad,
        gain_sums[1],
        feed_gate_out,
        feed_up_out,
        feed_down_out,
    )


def solution(mesh):
    token_spec = P(("dp", "row"), "col")
    weight_in, weight_out = P("col", "row"), P("row", "col")
    channel, channel_rows = P(("row", "col")), P(("row", "col"), None)
    parameters = (
        P("col"),
        weight_in,
        weight_in,
        channel_rows,
        channel,
        channel_rows,
        P(None, ("row", "col")),
        channel,
        channel_rows,
        channel,
        weight_out,
        P("col"),
        weight_in,
        weight_in,
        weight_out,
    )
    return jax.shard_map(
        body,
        mesh=mesh,
        in_specs=(token_spec,) + parameters + (token_spec,),
        out_specs=(token_spec, token_spec) + parameters,
        check_vma=False,
    )
```

```python
import jax
import jax.numpy as jnp
import numpy as np
from jax import lax
from jax.experimental import pallas as pl
from jax.experimental.pallas import tpu as pltpu
from jax.sharding import PartitionSpec as P

STATE = 16
CONV = 4
DT_RANK = 128
LANES = 128
ROWS = 8
LOG2E = np.float32(np.log2(np.e))
LN2 = np.float32(np.log(2.0))

epsilon = 1e-05
contract_first = (((0,), (0,)), ((), ()))
contract_last = (((1,), (1,)), ((), ()))
contract_inner = (((1,), (0,)), ((), ()))


def sigmoid_linear(values):
    return values * jax.nn.sigmoid(values)


def sigmoid_slope(values):
    logistic = jax.nn.sigmoid(values)
    return logistic * (1.0 + values * (1.0 - logistic))


def product(multiplicand, multiplier, dims=contract_inner):
    return lax.dot_general(multiplicand, multiplier, dims, preferred_element_type=jnp.float32)


def low(values):
    return values.astype(jnp.bfloat16)


def swap(values, axis, distance):
    return lax.ppermute(
        values, axis, [(i, i ^ distance) for i in range(lax.axis_size(axis))]
    )


def shift(values, axis, distance):
    size = lax.axis_size(axis)
    pairs = [(i, i + distance) for i in range(size) if 0 <= i + distance < size]
    return lax.ppermute(values, axis, pairs)


def gather_by_swaps(values, axis_name, axis):
    size, length = lax.axis_size(axis_name), values.shape[axis]
    index = lax.axis_index(axis_name)
    shape = list(values.shape)
    shape[axis] = size * length
    joined = jnp.zeros(shape, values.dtype)
    for distance in range(size):
        part = swap(values, axis_name, distance) if distance else values
        joined = lax.dynamic_update_slice_in_dim(
            joined, part, (index ^ distance) * length, axis
        )
    return joined


def gather_blocks(values):
    return gather_by_swaps(values[None], "col", 0)


def scatter_by_swaps(values, axis_name, axis, dtype):
    size = lax.axis_size(axis_name)
    length = values.shape[axis] // size
    index = lax.axis_index(axis_name)

    def block(distance):
        return lax.dynamic_slice_in_dim(values, (index ^ distance) * length, length, axis)

    total = block(0).astype(jnp.float32)
    for distance in range(1, size):
        total = total + swap(block(distance).astype(dtype), axis_name, distance).astype(
            jnp.float32
        )
    return total


def by_swaps():
    return lax.axis_size("row") == 4


def block_order():
    return lax.axis_index("row") if by_swaps() else jnp.int32(0)


def row_gather(values):
    if by_swaps():
        return jnp.concatenate(
            [values] + [swap(values, "row", distance) for distance in range(1, 4)], axis=0
        )
    return lax.all_gather(values, "row", axis=0, tiled=True)


def row_scatter(values):
    if by_swaps():
        count = values.shape[0] // 4
        total = values[:count]
        for distance in range(1, 4):
            block = low(values[distance * count : (distance + 1) * count])
            total = total + swap(block, "row", distance).astype(jnp.float32)
        return total
    return lax.psum_scatter(low(values), "row", scatter_dimension=0, tiled=True).astype(
        jnp.float32
    )


def row_total(values, local=None):
    if by_swaps():
        blocks = values.reshape((4, -1) + values.shape[1:])
        total = (values if local is None else local).reshape(blocks.shape)
        for distance in range(1, 4):
            got = swap(values, "row", distance).reshape(blocks.shape)
            total = total + jnp.concatenate(
                [got[k ^ distance : (k ^ distance) + 1] for k in range(4)], axis=0
            )
        return total.reshape(values.shape)
    return lax.psum(values, "row")


def block_moves():
    rows, cols = lax.axis_size("row"), lax.axis_size("col")
    return [(k, (k % rows) * cols + k // rows) for k in range(rows * cols)]


def exchange(pieces, axis_name):
    index = lax.axis_index(axis_name)
    joined = jnp.zeros_like(pieces)
    for distance in range(lax.axis_size(axis_name)):
        part = lax.dynamic_slice_in_dim(pieces, index ^ distance, 1, 0)
        if distance:
            part = swap(part, axis_name, distance)
        joined = lax.dynamic_update_slice_in_dim(joined, part, index ^ distance, 0)
    return joined


def to_whole_features(values):
    rows, cols = lax.axis_size("row"), lax.axis_size("col")
    if rows == cols:
        count, features = values.shape
        pieces = values.reshape(rows, count // rows, features)
        pieces = exchange(exchange(pieces, "row"), "col")
        return jnp.concatenate([pieces[c] for c in range(cols)], axis=1)
    split = lax.all_to_all(values, "col", split_axis=0, concat_axis=1, tiled=True)
    return lax.ppermute(split, ("row", "col"), block_moves())


def to_feature_blocks(arrays, others):
    rows, cols = lax.axis_size("row"), lax.axis_size("col")
    count, features = arrays[0].shape[0], arrays[0].shape[1] // cols
    if rows == cols:
        pieces = jnp.stack(
            [
                jnp.concatenate(
                    [values[:, c * features : (c + 1) * features] for values in arrays]
                )
                for c in range(cols)
            ]
        )
        pieces = lax.all_to_all(pieces, "col", split_axis=0, concat_axis=0)
        pieces, others = lax.optimization_barrier((pieces, others))
        pieces = exchange(pieces, "row")
        return [
            pieces[:, i * count : (i + 1) * count].reshape(rows * count, features)
            for i in range(len(arrays))
        ], others
    back = [(target, source) for source, target in block_moves()]

    def one(values):
        split = lax.ppermute(values, ("row", "col"), back)
        return lax.all_to_all(split, "col", split_axis=1, concat_axis=0, tiled=True)

    return [one(values) for values in arrays], others


def gather_weight(weight):
    half = weight.shape[0] // lax.axis_size("dp")
    part = lax.dynamic_slice_in_dim(weight, lax.axis_index("dp") * half, half, 0)
    return lax.all_gather(low(part), ("col", "dp"), axis=0, tiled=True)


def block_at(blocks, place):
    return lax.dynamic_index_in_dim(blocks, place, 0, keepdims=False)


def neighbours(outside, blocks, order, direction):
    last = blocks.shape[0] - 1
    edge = 0 if direction == -1 else last
    got = []
    for place in range(last + 1):
        own = place ^ order
        near = block_at(blocks, jnp.clip(own + direction, 0, last) ^ order)
        got.append(jnp.where(own == edge, outside, near))
    return jnp.stack(got)


def feature_halves(values):
    blocks, first = lax.axis_size("col"), lax.axis_index("dp") == 0
    half = values.shape[1] // (2 * blocks)
    parts = [values[:, i * half : (i + 1) * half] for i in range(2 * blocks)]
    upper, lower = jnp.concatenate(parts[0::2], axis=1), jnp.concatenate(parts[1::2], axis=1)
    return jnp.where(first, upper, lower), jnp.where(first, lower, upper)


def add_pair(own, other):
    return low(own + swap(other, "dp", 1).astype(jnp.float32))


def scatter_gradient(gradient):
    return lax.psum_scatter(gradient, "col", scatter_dimension=0, tiled=True)


def both_halves(own, axis):
    other = swap(own, "dp", 1)
    first = lax.axis_index("dp") == 0
    return jnp.concatenate(
        [jnp.where(first, own, other), jnp.where(first, other, own)], axis=axis
    )


def fold_rows(parts):
    row = lax.broadcasted_iota(jnp.int32, parts[0].shape, 0)
    for half in (1, 2, 4):
        mask = (row & half) == 0
        parts = [
            jnp.where(mask, a, b) + pltpu.roll(jnp.where(mask, b, a), ROWS - half, 0)
            for a, b in zip(parts[0::2], parts[1::2])
        ]
    return parts[0]


def spread(ref, token):
    return ref[pl.ds(token, ROWS, stride=0), :]


class Tiling:
    def __init__(self, order, tokens, channels, backward):
        self.order = order
        groups = channels // LANES
        self.tokens, self.channels = tokens, channels
        self.per = min(8, groups)
        self.block = min(tokens // lax.axis_size("row") if by_swaps() else 128, tokens)
        self.blocks = tokens // self.block
        self.grid = (groups // self.per, self.blocks)
        self.width = self.per * LANES
        self.backward = backward
        self.lanes = [slice(g * LANES, (g + 1) * LANES) for g in range(self.per)]

    def at(self, b):
        return self.blocks - 1 - b if self.backward else b

    def narrow(self):
        def spec(i):
            return pl.BlockSpec(
                (self.block, LANES), lambda g, b, order: (self.at(b) ^ order[0], g * self.per + i)
            )

        return [spec(i) for i in range(self.per)]

    def token_spec(self):
        return pl.BlockSpec(
            (self.block, self.width), lambda g, b, order: (self.at(b) ^ order[0], g)
        )

    def wide_spec(self):
        return pl.BlockSpec(
            (self.block, STATE, LANES), lambda g, b, order: (self.at(b) ^ order[0], 0, 0)
        )

    def state_spec(self):
        return pl.BlockSpec((STATE, self.width), lambda g, b, order: (0, g))

    def history_spec(self):
        return pl.BlockSpec(
            (self.block, STATE, self.width), lambda g, b, order: (self.at(b), 0, g)
        )

    def part_spec(self):
        return pl.BlockSpec(
            (1, self.block, LANES), lambda g, b, order: (g, self.at(b) ^ order[0], 0)
        )

    def load(self, ref):
        out = []
        for lanes in self.lanes:
            out += [ref[0:8, lanes], ref[8:16, lanes]]
        return tuple(out)

    def store(self, ref, values):
        for g, lanes in enumerate(self.lanes):
            ref[0:8, lanes] = values[2 * g]
            ref[8:16, lanes] = values[2 * g + 1]

    def call(self, kernel, name, in_specs, out_specs, out_shape, scratch=()):
        call = pl.pallas_call(
            kernel,
            out_shape=out_shape,
            grid_spec=pltpu.PrefetchScalarGridSpec(
                num_scalar_prefetch=1,
                grid=self.grid,
                in_specs=in_specs,
                out_specs=out_specs,
                scratch_shapes=list(scratch),
            ),
            compiler_params=pltpu.CompilerParams(
                dimension_semantics=("arbitrary", "arbitrary"),
                vmem_limit_bytes=56 * 2**20,
            ),
            name=name,
        )
        return lambda *operands: call(self.order.reshape(1), *operands)


def pair(ref, token):
    return ref[token, 0:8, :], ref[token, 8:16, :]


def f32(*shape):
    return jax.ShapeDtypeStruct(shape, jnp.float32)


def chunk_state(order, step, drive, wide, rate, backward):
    t = Tiling(order, *step.shape, backward)
    per = t.per

    def kernel(_, *refs):
        step_refs, drive_refs = refs[:per], refs[per : 2 * per]
        wide_ref, rate_ref, state_ref = refs[2 * per :]

        @pl.when(pl.program_id(1) == 0)
        def _():
            state_ref[...] = jnp.zeros_like(state_ref)

        rates = t.load(rate_ref)

        def some(i, state):
            state = list(state)
            base = t.block - ROWS - i * ROWS if backward else i * ROWS
            for j in range(ROWS - 1, -1, -1) if backward else range(ROWS):
                token = base + j
                wides = pair(wide_ref, token)
                for g in range(per):
                    now = spread(step_refs[g], token)
                    force = spread(drive_refs[g], token)
                    for k in (0, 1):
                        m = 2 * g + k
                        factor = jnp.exp2(now * rates[m])
                        if backward:
                            state[m] = factor * (state[m] + force * wides[k])
                        else:
                            state[m] = factor * state[m] + force * wides[k]
            return tuple(state)

        t.store(
            state_ref, lax.fori_loop(0, t.block // ROWS, some, t.load(state_ref))
        )

    return t.call(
        kernel,
        "chunk_state_back" if backward else "chunk_state",
        t.narrow() + t.narrow() + [t.wide_spec(), t.state_spec()],
        t.state_spec(),
        f32(STATE, t.channels),
    )(*[step] * per, *[drive] * per, wide, rate)


def scan_forward(order, step, drive, in_wide, out_wide, rate, entry):
    t = Tiling(order, *step.shape, False)
    per = t.per

    def kernel(_, *refs):
        step_refs, drive_refs = refs[:per], refs[per : 2 * per]
        in_ref, out_ref, rate_ref, entry_ref, y_ref, before_ref, last_ref = refs[2 * per :]

        @pl.when(pl.program_id(1) == 0)
        def _():
            last_ref[...] = entry_ref[...]

        rates = t.load(rate_ref)

        def some(i, state):
            state = list(state)
            base = pl.multiple_of(i * ROWS, ROWS)
            sums = [[None] * ROWS for _ in range(per)]
            for j in range(ROWS):
                token = base + j
                ins, outs = pair(in_ref, token), pair(out_ref, token)
                for g in range(per):
                    now = spread(step_refs[g], token)
                    force = spread(drive_refs[g], token)
                    total = None
                    for k in (0, 1):
                        m = 2 * g + k
                        before_ref[token, 8 * k : 8 * k + 8, t.lanes[g]] = state[m]
                        state[m] = jnp.exp2(now * rates[m]) * state[m] + force * ins[k]
                        term = state[m] * outs[k]
                        total = term if total is None else total + term
                    sums[g][j] = total
            for g in range(per):
                y_ref[pl.ds(base, ROWS), t.lanes[g]] = fold_rows(sums[g])
            return tuple(state)

        t.store(last_ref, lax.fori_loop(0, t.block // ROWS, some, t.load(last_ref)))

    return t.call(
        kernel,
        "scan_forward",
        t.narrow()
        + t.narrow()
        + [t.wide_spec(), t.wide_spec(), t.state_spec(), t.state_spec()],
        (t.token_spec(), t.history_spec(), t.state_spec()),
        (
            f32(t.tokens, t.channels),
            f32(t.tokens, STATE, t.channels),
            f32(STATE, t.channels),
        ),
    )(*[step] * per, *[drive] * per, in_wide, out_wide, rate, entry)


def scan_backward(order, step, drive, back, in_wide, out_wide, rate, entry, before, last):
    t = Tiling(order, *step.shape, True)
    per = t.per

    def kernel(_, *refs):
        step_refs, drive_refs, back_refs = (refs[i * per : (i + 1) * per] for i in range(3))
        in_ref, out_ref, rate_ref, entry_ref, before_ref, last_ref = refs[
            3 * per : 3 * per + 6
        ]
        rate_sum_ref, in_sum_ref, decay_ref, coefficient_ref = refs[3 * per + 6 : 3 * per + 10]
        carry_ref, state_ref, in_part_ref, out_part_ref = refs[3 * per + 10 :]

        @pl.when(pl.program_id(1) == 0)
        def _():
            decay_ref[...] = jnp.zeros_like(decay_ref)
            carry_ref[...] = entry_ref[...]
            state_ref[...] = last_ref[...]

        rates = t.load(rate_ref)

        def some(i, carried):
            carry, state, decay = (list(part) for part in carried)
            base = pl.multiple_of(t.block - ROWS - i * ROWS, ROWS)
            rate_sums = [[None] * ROWS for _ in range(per)]
            in_sums = [[None] * ROWS for _ in range(per)]
            for j in range(ROWS - 1, -1, -1):
                token = base + j
                ins, outs = pair(in_ref, token), pair(out_ref, token)
                in_part, out_part = [None, None], [None, None]
                for g in range(per):
                    now = spread(step_refs[g], token)
                    force = spread(drive_refs[g], token)
                    above = spread(back_refs[g], token)
                    by_rate, by_in = [None, None], [None, None]
                    for k in (0, 1):
                        m = 2 * g + k
                        earlier = before_ref[token, 8 * k : 8 * k + 8, t.lanes[g]]
                        grad = carry[m] + above * outs[k]
                        carry[m] = jnp.exp2(now * rates[m]) * grad
                        weighted = carry[m] * earlier
                        decay[m] = decay[m] + weighted * now
                        by_rate[k] = weighted * rates[m]
                        by_in[k] = grad * ins[k]
                        for parts, term in (
                            (in_part, grad * force),
                            (out_part, above * state[m]),
                        ):
                            parts[k] = term if parts[k] is None else parts[k] + term
                        state[m] = earlier
                    rate_sums[g][j] = by_rate[0] + by_rate[1]
                    in_sums[g][j] = by_in[0] + by_in[1]
                for k in (0, 1):
                    place = pl.multiple_of(token * STATE + k * ROWS, ROWS)
                    in_part_ref[pl.ds(place, ROWS), :] = in_part[k]
                    out_part_ref[pl.ds(place, ROWS), :] = out_part[k]
            for g in range(per):
                rate_sum_ref[pl.ds(base, ROWS), t.lanes[g]] = fold_rows(rate_sums[g])
                in_sum_ref[pl.ds(base, ROWS), t.lanes[g]] = fold_rows(in_sums[g])
            return tuple(carry), tuple(state), tuple(decay)

        carry, state, decay = lax.fori_loop(
            0,
            t.block // ROWS,
            some,
            (t.load(carry_ref), t.load(state_ref), t.load(decay_ref)),
        )
        t.store(carry_ref, carry)
        t.store(state_ref, state)
        t.store(decay_ref, decay)

        for part_ref in (in_part_ref, out_part_ref):
            part = part_ref[...]
            high = low(part)
            ones = jnp.ones((LANES, LANES), jnp.bfloat16)
            part_ref[...] = product(high, ones) + product(
                low(part - high.astype(jnp.float32)), ones
            )
        row = lax.broadcasted_iota(jnp.int32, (ROWS, LANES), 0)
        lane = lax.broadcasted_iota(jnp.int32, (ROWS, LANES), 1)

        def gathered(i, _):
            base = pl.multiple_of(i * ROWS, ROWS)
            tokens = []
            for j in range(ROWS):
                total = None
                for m, part_ref in ((0, in_part_ref), (1, out_part_ref)):
                    for k in (0, 1):
                        place = pl.multiple_of((base + j) * STATE + k * ROWS, ROWS)
                        term = jnp.where(
                            lane == row + (m * STATE + k * ROWS),
                            part_ref[pl.ds(place, ROWS), :],
                            0.0,
                        )
                        total = term if total is None else total + term
                tokens.append(total)
            coefficient_ref[0, pl.ds(base, ROWS), :] = fold_rows(tokens)
            return _

        lax.fori_loop(0, t.block // ROWS, gathered, 0)

    rate_sum, in_sum, decay, coefficients = t.call(
        kernel,
        "scan_backward",
        t.narrow()
        + t.narrow()
        + t.narrow()
        + [
            t.wide_spec(),
            t.wide_spec(),
            t.state_spec(),
            t.state_spec(),
            t.history_spec(),
            t.state_spec(),
        ],
        (t.token_spec(), t.token_spec(), t.state_spec(), t.part_spec()),
        (
            f32(t.tokens, t.channels),
            f32(t.tokens, t.channels),
            f32(STATE, t.channels),
            f32(t.grid[0], t.tokens, LANES),
        ),
        [pltpu.VMEM((STATE, t.width), jnp.float32)] * 2
        + [pltpu.VMEM((t.block * STATE, LANES), jnp.float32)] * 2,
    )(
        *[step] * per,
        *[drive] * per,
        *[back] * per,
        in_wide,
        out_wide,
        rate,
        entry,
        before,
        last,
    )
    return rate_sum, in_sum, decay, jnp.sum(coefficients, 0)[:, : 2 * STATE]


def neighbour_totals(step_total, direction):
    return [
        shift(step_total, "col", direction * distance)
        for distance in range(1, lax.axis_size("col") - 1)
    ]


def chunk_entry(state, totals, rate, direction):
    last = lax.axis_size("col") - 1
    entry = None
    for distance in range(last, 0, -1):
        got = shift(low(state), "col", direction * distance).astype(jnp.float32)
        if entry is not None:
            got = got + jnp.exp2(totals[distance - 1] * rate) * entry
        entry = got
    return entry


def widen(coefficients):
    return jnp.broadcast_to(coefficients[:, :, None], coefficients.shape + (LANES,))


def norm_forward(values, weights):
    inverse = lax.rsqrt(jnp.mean(values * values, axis=1, keepdims=True) + epsilon)
    scaled = values * inverse
    return scaled, inverse, low(scaled * weights)


def norm_backward(upstream, scaled, inverse, weights):
    weighted = upstream * weights
    inner_mean = jnp.mean(weighted * scaled, axis=1, keepdims=True)
    return (
        inverse * (weighted - scaled * inner_mean),
        jnp.sum(upstream * scaled, axis=0, keepdims=True),
    )


def body(
    tokens,
    mixer_norm,
    in_value,
    in_gate,
    conv_weight,
    conv_bias,
    state_proj,
    step_proj,
    step_bias,
    decay_log,
    skip_gain,
    mixer_out,
    feed_norm,
    feed_gate,
    feed_up,
    feed_down,
    out_grad,
):
    channels, units = in_value.shape[1], feed_gate.shape[1]
    order = block_order()
    rows, index = lax.axis_size("row"), lax.axis_index("dp")
    first = gather_weight(jnp.concatenate([in_value, in_gate, mixer_out.T], axis=1))
    in_low, mixer_low = first[:, : 2 * channels], first[:, 2 * channels :]
    feed_low = gather_weight(jnp.concatenate([feed_gate, feed_up], axis=1))
    feed_down_low = gather_weight(feed_down.T)

    inputs = to_whole_features(tokens)
    own_channels = conv_bias.shape[0]
    gains = jnp.stack([mixer_norm, feed_norm]).reshape(-1, own_channels)
    packed = jnp.concatenate(
        [
            gains,
            conv_weight.T,
            conv_bias[None],
            step_bias[None],
            skip_gain[None],
            decay_log.T,
        ],
        axis=0,
    )
    packed = gather_blocks(packed)
    gain_rows = gains.shape[0]
    gains = packed[:, :gain_rows].reshape(-1, 2, mixer_norm.shape[0])
    mixer_gain = gains[:, 0].reshape(1, -1)
    feed_gain = gains[:, 1].reshape(1, -1)
    packed = jnp.swapaxes(packed[:, gain_rows:], 0, 1).reshape(-1, channels)
    taps = packed[:CONV]
    conv_bias_row, step_bias_row, skip_row = (
        packed[CONV + i : CONV + i + 1] for i in range(3)
    )
    decay_rate = -jnp.exp(packed[CONV + 3 :])
    projections = jnp.concatenate([low(step_proj), low(state_proj).T], axis=0)
    projections, inputs = lax.optimization_barrier((projections, inputs))
    half = projections.shape[0] // 2
    projections = gather_blocks(
        lax.dynamic_slice_in_dim(projections, index * half, half, 0)
    )
    projections = both_halves(projections, 1)
    projections = jnp.swapaxes(projections, 0, 1).reshape(-1, channels)
    step_weight, state_low = projections[:DT_RANK], projections[DT_RANK:]
    inputs = inputs.astype(jnp.float32)

    scaled_first, inverse_first, normed_first = norm_forward(inputs, mixer_gain)
    normed_all = row_gather(normed_first)
    count = normed_all.shape[0]
    both_in = product(normed_all, in_low)
    both_in, out_grad = lax.optimization_barrier((both_in, out_grad))
    out_back_low = to_whole_features(out_grad)
    grad_all = row_gather(out_back_low)
    mixer_in, gate_in = both_in[:, :channels], both_in[:, channels:]
    mixer_in = mixer_in.reshape(rows, -1, channels)
    length = mixer_in.shape[1]
    tails = mixer_in[:, -ROWS:]
    outside = shift(block_at(tails, (rows - 1) ^ order), "col", 1)
    earlier = neighbours(outside, tails, order, -1)
    padded = jnp.concatenate([earlier[:, ROWS - CONV + 1 :], mixer_in], axis=1)
    conv_out = conv_bias_row + sum(
        padded[:, k : k + length] * taps[k : k + 1] for k in range(CONV)
    ).reshape(count, channels)
    conv_act = low(sigmoid_linear(conv_out))
    projected = row_total(product(conv_act, state_low, contract_last))
    step_low = low(projected[:, :DT_RANK])
    in_wide = widen(projected[:, DT_RANK : DT_RANK + STATE])
    out_wide = widen(projected[:, DT_RANK + STATE :])
    step_pre = product(step_low, step_weight) + step_bias_row
    step_size = jax.nn.softplus(step_pre)
    act_float = conv_act.astype(jnp.float32)
    drive = step_size * act_float
    rate = decay_rate * LOG2E
    step_total = jnp.sum(step_size, axis=0, keepdims=True)
    earlier_totals = neighbour_totals(step_total, 1)
    later_totals = neighbour_totals(step_total, -1)
    handed = chunk_state(order, step_size, drive, in_wide, rate, False)
    entry = chunk_entry(handed, earlier_totals, rate, 1)
    entry, later_totals = lax.optimization_barrier((entry, later_totals))
    scanned, before, last = scan_forward(
        order, step_size, drive, in_wide, out_wide, rate, entry
    )
    scan_out = scanned + skip_row * act_float
    gate_act = sigmoid_linear(gate_in)
    gated = low(scan_out * gate_act)
    middle = inputs + row_scatter(product(gated, mixer_low, contract_last))

    scaled_second, inverse_second, normed_second = norm_forward(middle, feed_gain)
    normed_feed = row_gather(normed_second)
    both_pre = product(normed_feed, feed_low)
    gate_pre, up_pre = both_pre[:, :units], both_pre[:, units:]
    gate_swish = sigmoid_linear(gate_pre)
    hidden = low(gate_swish * up_pre)
    grad_own, grad_other = feature_halves(grad_all)
    down_grad = add_pair(
        product(grad_own, hidden, contract_first),
        low(product(grad_other, hidden, contract_first)),
    )
    feed_down_low, down_grad = lax.optimization_barrier((feed_down_low, down_grad))
    down_own = scatter_gradient(down_grad)

    hidden_back = product(grad_all, feed_down_low)
    gate_back = low(hidden_back * up_pre * sigmoid_slope(gate_pre))
    up_back = low(hidden_back * gate_swish)
    both_back = jnp.concatenate([gate_back, up_back], axis=1)
    feed_left, feed_right = feature_halves(normed_feed)
    other_grad = low(product(feed_right, both_back, contract_first))
    both_back, other_grad = lax.optimization_barrier((both_back, other_grad))
    normed_back = product(both_back, feed_low, contract_last)
    feed_grad = add_pair(product(feed_left, both_back, contract_first), other_grad)
    normed_back, feed_grad = lax.optimization_barrier((normed_back, feed_grad))
    feed_own = scatter_gradient(feed_grad)
    normed_back = row_scatter(normed_back)
    middle_norm, feed_norm_part = norm_backward(
        normed_back, scaled_second, inverse_second, feed_gain
    )
    middle_back = out_back_low.astype(jnp.float32) + middle_norm
    middle_low, down_own = lax.optimization_barrier((low(middle_back), down_own))
    middle_all = row_gather(middle_low)

    gated_back = product(middle_all, mixer_low)
    scan_back = gated_back * gate_act
    gate_in_back = low(gated_back * scan_out * sigmoid_slope(gate_in))
    normed_own, normed_other = feature_halves(normed_all)
    middle_own, middle_other = feature_halves(middle_all)
    pair_own = jnp.concatenate(
        [
            product(middle_own, gated, contract_first),
            product(normed_own, gate_in_back, contract_first),
        ],
        axis=1,
    )
    pair_other = jnp.concatenate(
        [
            low(product(middle_other, gated, contract_first)),
            low(product(normed_other, gate_in_back, contract_first)),
        ],
        axis=1,
    )
    scan_back, hidden, pair_other = lax.optimization_barrier((scan_back, hidden, pair_other))
    pair_grad = add_pair(pair_own, pair_other)
    output = low(middle + row_scatter(product(hidden, feed_down_low, contract_last)))
    handed_back = chunk_state(order, step_size, scan_back, out_wide, rate, True)
    entry_back = chunk_entry(handed_back, later_totals, rate, -1)
    rate_sum, in_sum, decay_sum, coefficient_back = scan_backward(
        order,
        step_size,
        drive,
        scan_back,
        in_wide,
        out_wide,
        rate,
        entry_back,
        before,
        last,
    )
    rate_sum, in_sum, coefficient_back, pair_grad, output = lax.optimization_barrier(
        (rate_sum, in_sum, coefficient_back, pair_grad, output)
    )
    step_back = rate_sum * LN2 + act_float * in_sum
    act_scan = step_size * in_sum + skip_row * scan_back
    pre_back = step_back * jax.nn.sigmoid(step_pre)
    pre_low = low(pre_back)
    rank_back = product(pre_low, step_weight, contract_last)
    partial = jnp.concatenate([rank_back, coefficient_back], axis=1)
    local, pair_grad, feed_own = lax.optimization_barrier((partial, pair_grad, feed_own))
    proj_back = low(row_total(partial, local))
    pair_own = scatter_gradient(pair_grad)
    act_back = act_scan + product(proj_back, state_low)
    conv_back = act_back * sigmoid_slope(conv_out)
    conv_blocks = conv_back.reshape(rows, length, channels)
    heads = conv_blocks[:, :ROWS]
    outside = shift(block_at(heads, order), "col", -1)
    later = neighbours(outside, heads, order, 1)
    trailing = jnp.concatenate([conv_blocks, later[:, : CONV - 1]], axis=1)
    mixer_back = low(
        sum(
            trailing[:, CONV - 1 - k : CONV - 1 - k + length] * taps[k : k + 1]
            for k in range(CONV)
        )
    ).reshape(count, channels)
    both_in_back = jnp.concatenate([mixer_back, gate_in_back], axis=1)
    normed_first_back = product(both_in_back, in_low, contract_last)
    mixer_back, normed_first_back = lax.optimization_barrier((mixer_back, normed_first_back))
    in_value_grad = add_pair(
        product(normed_own, mixer_back, contract_first),
        low(product(normed_other, mixer_back, contract_first)),
    )
    input_norm, mixer_norm_part = norm_backward(
        row_scatter(normed_first_back), scaled_first, inverse_first, mixer_gain
    )
    tokens_grad = low(middle_back + input_norm)

    def whole(own, after):
        own, _ = lax.optimization_barrier((own, after))
        return both_halves(own, 0)

    feed_grad = whole(feed_own, proj_back)
    down_grad = whole(down_own, proj_back)
    finished = (
        feed_grad[:, :units].astype(jnp.float32),
        feed_grad[:, units:].astype(jnp.float32),
        down_grad.T.astype(jnp.float32),
    )
    gain_parts = jnp.concatenate([mixer_norm_part, feed_norm_part], axis=0)
    in_value_grad, pair_own, tokens_grad, output, gain_parts, *finished = (
        lax.optimization_barrier(
            (in_value_grad, pair_own, tokens_grad, output, gain_parts) + finished
        )
    )
    feed_gate_out, feed_up_out, feed_down_out = finished
    pair_grad = both_halves(pair_own, 0)
    finished = (
        pair_grad[:, channels:].astype(jnp.float32),
        pair_grad[:, :channels].T.astype(jnp.float32),
    )

    def over_tokens(values):
        return jnp.sum(values, axis=0, keepdims=True)

    gain_parts = gain_parts.reshape(2, lax.axis_size("col"), -1, own_channels)
    gain_parts = jnp.swapaxes(gain_parts, 1, 2).reshape(gain_rows, channels)
    packed_grad = jnp.concatenate(
        [gain_parts]
        + [
            jnp.sum(conv_blocks * padded[:, k : k + length], axis=(0, 1))[None]
            for k in range(CONV)
        ]
        + [
            over_tokens(conv_back),
            over_tokens(pre_back),
            over_tokens(scan_back * act_float),
            decay_sum * decay_rate,
        ],
        axis=0,
    )
    projection_grad = jnp.concatenate(
        [
            product(step_low, pre_low, contract_first),
            product(proj_back, conv_act, contract_first),
        ],
        axis=0,
    )
    (output, tokens_grad), (packed_grad, projection_grad, in_value_grad) = to_feature_blocks(
        (output, tokens_grad), (packed_grad, projection_grad, in_value_grad)
    )
    value_own = scatter_gradient(in_value_grad)

    half = projection_grad.shape[0] // 2
    mine, others = (
        lax.dynamic_slice_in_dim(projection_grad, place * half, half, 0)
        for place in (index, 1 - index)
    )
    small = jnp.concatenate(
        [mine + swap(others, "dp", 1), packed_grad + swap(packed_grad, "dp", 1)], axis=0
    )
    small = scatter_by_swaps(small, "col", 1, jnp.bfloat16)
    projection_grad = both_halves(small[:half], 0)
    packed_grad = small[half:]
    gain_sums = packed_grad[:gain_rows]
    distance = 1
    while distance < rows:
        gain_sums = gain_sums + swap(gain_sums, "row", distance)
        distance *= 2
    gain_sums = gain_sums.reshape(2, -1)
    packed_grad = packed_grad[gain_rows:]
    value_own, *finished = lax.optimization_barrier((value_own,) + finished)
    gate_out, mixer_out_grad = finished
    return (
        output,
        tokens_grad.astype(jnp.float32),
        gain_sums[0],
        both_halves(value_own, 0).astype(jnp.float32),
        gate_out,
        packed_grad[:CONV].T,
        packed_grad[CONV],
        projection_grad[DT_RANK:].T,
        projection_grad[:DT_RANK],
        packed_grad[CONV + 1],
        packed_grad[CONV + 3 :].T,
        packed_grad[CONV + 2],
        mixer_out_grad,
        gain_sums[1],
        feed_gate_out,
        feed_up_out,
        feed_down_out,
    )


def solution(mesh):
    token_spec = P(("dp", "row"), "col")
    weight_in, weight_out = P("col", "row"), P("row", "col")
    channel, channel_rows = P(("row", "col")), P(("row", "col"), None)
    parameters = (
        P("col"),
        weight_in,
        weight_in,
        channel_rows,
        channel,
        channel_rows,
        P(None, ("row", "col")),
        channel,
        channel_rows,
        channel,
        weight_out,
        P("col"),
        weight_in,
        weight_in,
        weight_out,
    )
    return jax.shard_map(
        body,
        mesh=mesh,
        in_specs=(token_spec,) + parameters + (token_spec,),
        out_specs=(token_spec, token_spec) + parameters,
        check_vma=False,
    )
```

```python
import jax
import jax.numpy as jnp
import numpy as np
from jax import lax
from jax.experimental import pallas as pl
from jax.experimental.pallas import tpu as pltpu
from jax.sharding import PartitionSpec as P

STATE = 16
CONV = 4
DT_RANK = 128
LANES = 128
ROWS = 8
LOG2E = np.float32(np.log2(np.e))
LN2 = np.float32(np.log(2.0))

epsilon = 1e-05
contract_first = (((0,), (0,)), ((), ()))
contract_last = (((1,), (1,)), ((), ()))
contract_inner = (((1,), (0,)), ((), ()))


def sigmoid_linear(values):
    return values * jax.nn.sigmoid(values)


def sigmoid_slope(values):
    logistic = jax.nn.sigmoid(values)
    return logistic * (1.0 + values * (1.0 - logistic))


def product(multiplicand, multiplier, dims=contract_inner):
    return lax.dot_general(multiplicand, multiplier, dims, preferred_element_type=jnp.float32)


def low(values):
    return values.astype(jnp.bfloat16)


def swap(values, axis, distance):
    return lax.ppermute(
        values, axis, [(i, i ^ distance) for i in range(lax.axis_size(axis))]
    )


def shift(values, axis, distance):
    size = lax.axis_size(axis)
    pairs = [(i, i + distance) for i in range(size) if 0 <= i + distance < size]
    return lax.ppermute(values, axis, pairs)


def gather_by_swaps(values, axis_name, axis):
    size, length = lax.axis_size(axis_name), values.shape[axis]
    index = lax.axis_index(axis_name)
    shape = list(values.shape)
    shape[axis] = size * length
    joined = jnp.zeros(shape, values.dtype)
    for distance in range(size):
        part = swap(values, axis_name, distance) if distance else values
        joined = lax.dynamic_update_slice_in_dim(
            joined, part, (index ^ distance) * length, axis
        )
    return joined


def gather_blocks(values):
    return gather_by_swaps(values[None], "col", 0)


def scatter_by_swaps(values, axis_name, axis, dtype):
    size = lax.axis_size(axis_name)
    length = values.shape[axis] // size
    index = lax.axis_index(axis_name)

    def block(distance):
        return lax.dynamic_slice_in_dim(values, (index ^ distance) * length, length, axis)

    total = block(0).astype(jnp.float32)
    for distance in range(1, size):
        total = total + swap(block(distance).astype(dtype), axis_name, distance).astype(
            jnp.float32
        )
    return total


def by_swaps():
    return lax.axis_size("row") == 4


def block_order():
    return lax.axis_index("row") if by_swaps() else jnp.int32(0)


def row_gather(values):
    if by_swaps():
        return jnp.concatenate(
            [values] + [swap(values, "row", distance) for distance in range(1, 4)], axis=0
        )
    return lax.all_gather(values, "row", axis=0, tiled=True)


def row_scatter(values):
    if by_swaps():
        count = values.shape[0] // 4
        total = values[:count]
        for distance in range(1, 4):
            block = low(values[distance * count : (distance + 1) * count])
            total = total + swap(block, "row", distance).astype(jnp.float32)
        return total
    return lax.psum_scatter(low(values), "row", scatter_dimension=0, tiled=True).astype(
        jnp.float32
    )


def row_total(values, local=None):
    if by_swaps():
        blocks = values.reshape((4, -1) + values.shape[1:])
        total = (values if local is None else local).reshape(blocks.shape)
        for distance in range(1, 4):
            got = swap(values, "row", distance).reshape(blocks.shape)
            total = total + jnp.concatenate(
                [got[k ^ distance : (k ^ distance) + 1] for k in range(4)], axis=0
            )
        return total.reshape(values.shape)
    return lax.psum(values, "row")


def block_moves():
    rows, cols = lax.axis_size("row"), lax.axis_size("col")
    return [(k, (k % rows) * cols + k // rows) for k in range(rows * cols)]


def exchange(pieces, axis_name):
    index = lax.axis_index(axis_name)
    joined = jnp.zeros_like(pieces)
    for distance in range(lax.axis_size(axis_name)):
        part = lax.dynamic_slice_in_dim(pieces, index ^ distance, 1, 0)
        if distance:
            part = swap(part, axis_name, distance)
        joined = lax.dynamic_update_slice_in_dim(joined, part, index ^ distance, 0)
    return joined


def to_whole_features(values):
    rows, cols = lax.axis_size("row"), lax.axis_size("col")
    if rows == cols:
        count, features = values.shape
        pieces = values.reshape(rows, count // rows, features)
        pieces = lax.all_to_all(exchange(pieces, "row"), "col", split_axis=0, concat_axis=0)
        return jnp.concatenate([pieces[c] for c in range(cols)], axis=1)
    split = lax.all_to_all(values, "col", split_axis=0, concat_axis=1, tiled=True)
    return lax.ppermute(split, ("row", "col"), block_moves())


def to_feature_blocks(arrays, others):
    rows, cols = lax.axis_size("row"), lax.axis_size("col")
    count, features = arrays[0].shape[0], arrays[0].shape[1] // cols
    if rows == cols:
        pieces = jnp.stack(
            [
                jnp.concatenate(
                    [values[:, c * features : (c + 1) * features] for values in arrays]
                )
                for c in range(cols)
            ]
        )
        pieces = lax.all_to_all(pieces, "col", split_axis=0, concat_axis=0)
        pieces, others = lax.optimization_barrier((pieces, others))
        pieces = exchange(pieces, "row")
        return [
            pieces[:, i * count : (i + 1) * count].reshape(rows * count, features)
            for i in range(len(arrays))
        ], others
    back = [(target, source) for source, target in block_moves()]

    def one(values):
        split = lax.ppermute(values, ("row", "col"), back)
        return lax.all_to_all(split, "col", split_axis=1, concat_axis=0, tiled=True)

    return [one(values) for values in arrays], others


def gather_weight(weight):
    half = weight.shape[0] // lax.axis_size("dp")
    part = lax.dynamic_slice_in_dim(weight, lax.axis_index("dp") * half, half, 0)
    return lax.all_gather(low(part), ("col", "dp"), axis=0, tiled=True)


def block_at(blocks, place):
    return lax.dynamic_index_in_dim(blocks, place, 0, keepdims=False)


def neighbours(outside, blocks, order, direction):
    last = blocks.shape[0] - 1
    edge = 0 if direction == -1 else last
    got = []
    for place in range(last + 1):
        own = place ^ order
        near = block_at(blocks, jnp.clip(own + direction, 0, last) ^ order)
        got.append(jnp.where(own == edge, outside, near))
    return jnp.stack(got)


def feature_halves(values):
    blocks, first = lax.axis_size("col"), lax.axis_index("dp") == 0
    half = values.shape[1] // (2 * blocks)
    parts = [values[:, i * half : (i + 1) * half] for i in range(2 * blocks)]
    upper, lower = jnp.concatenate(parts[0::2], axis=1), jnp.concatenate(parts[1::2], axis=1)
    return jnp.where(first, upper, lower), jnp.where(first, lower, upper)


def add_pair(own, other):
    return low(own + swap(other, "dp", 1).astype(jnp.float32))


def scatter_gradient(gradient):
    return lax.psum_scatter(gradient, "col", scatter_dimension=0, tiled=True)


def both_halves(own, axis):
    other = swap(own, "dp", 1)
    first = lax.axis_index("dp") == 0
    return jnp.concatenate(
        [jnp.where(first, own, other), jnp.where(first, other, own)], axis=axis
    )


def fold_rows(parts):
    row = lax.broadcasted_iota(jnp.int32, parts[0].shape, 0)
    for half in (1, 2, 4):
        mask = (row & half) == 0
        parts = [
            jnp.where(mask, a, b) + pltpu.roll(jnp.where(mask, b, a), ROWS - half, 0)
            for a, b in zip(parts[0::2], parts[1::2])
        ]
    return parts[0]


def spread(ref, token):
    return ref[pl.ds(token, ROWS, stride=0), :]


class Tiling:
    def __init__(self, order, tokens, channels, backward):
        self.order = order
        groups = channels // LANES
        self.tokens, self.channels = tokens, channels
        self.per = min(8, groups)
        self.block = min(tokens // lax.axis_size("row") if by_swaps() else 128, tokens)
        self.blocks = tokens // self.block
        self.grid = (groups // self.per, self.blocks)
        self.width = self.per * LANES
        self.backward = backward
        self.lanes = [slice(g * LANES, (g + 1) * LANES) for g in range(self.per)]

    def at(self, b):
        return self.blocks - 1 - b if self.backward else b

    def narrow(self):
        def spec(i):
            return pl.BlockSpec(
                (self.block, LANES), lambda g, b, order: (self.at(b) ^ order[0], g * self.per + i)
            )

        return [spec(i) for i in range(self.per)]

    def token_spec(self):
        return pl.BlockSpec(
            (self.block, self.width), lambda g, b, order: (self.at(b) ^ order[0], g)
        )

    def wide_spec(self):
        return pl.BlockSpec(
            (self.block, STATE, LANES), lambda g, b, order: (self.at(b) ^ order[0], 0, 0)
        )

    def state_spec(self):
        return pl.BlockSpec((STATE, self.width), lambda g, b, order: (0, g))

    def history_spec(self):
        return pl.BlockSpec(
            (self.block, STATE, self.width), lambda g, b, order: (self.at(b), 0, g)
        )

    def part_spec(self):
        return pl.BlockSpec(
            (1, self.block, LANES), lambda g, b, order: (g, self.at(b) ^ order[0], 0)
        )

    def load(self, ref):
        out = []
        for lanes in self.lanes:
            out += [ref[0:8, lanes], ref[8:16, lanes]]
        return tuple(out)

    def store(self, ref, values):
        for g, lanes in enumerate(self.lanes):
            ref[0:8, lanes] = values[2 * g]
            ref[8:16, lanes] = values[2 * g + 1]

    def call(self, kernel, name, in_specs, out_specs, out_shape, scratch=()):
        call = pl.pallas_call(
            kernel,
            out_shape=out_shape,
            grid_spec=pltpu.PrefetchScalarGridSpec(
                num_scalar_prefetch=1,
                grid=self.grid,
                in_specs=in_specs,
                out_specs=out_specs,
                scratch_shapes=list(scratch),
            ),
            compiler_params=pltpu.CompilerParams(
                dimension_semantics=("arbitrary", "arbitrary"),
                vmem_limit_bytes=56 * 2**20,
            ),
            name=name,
        )
        return lambda *operands: call(self.order.reshape(1), *operands)


def pair(ref, token):
    return ref[token, 0:8, :], ref[token, 8:16, :]


def f32(*shape):
    return jax.ShapeDtypeStruct(shape, jnp.float32)


def chunk_state(order, step, drive, wide, rate, backward):
    t = Tiling(order, *step.shape, backward)
    per = t.per

    def kernel(_, *refs):
        step_refs, drive_refs = refs[:per], refs[per : 2 * per]
        wide_ref, rate_ref, state_ref = refs[2 * per :]

        @pl.when(pl.program_id(1) == 0)
        def _():
            state_ref[...] = jnp.zeros_like(state_ref)

        rates = t.load(rate_ref)

        def some(i, state):
            state = list(state)
            base = t.block - ROWS - i * ROWS if backward else i * ROWS
            for j in range(ROWS - 1, -1, -1) if backward else range(ROWS):
                token = base + j
                wides = pair(wide_ref, token)
                for g in range(per):
                    now = spread(step_refs[g], token)
                    force = spread(drive_refs[g], token)
                    for k in (0, 1):
                        m = 2 * g + k
                        factor = jnp.exp2(now * rates[m])
                        if backward:
                            state[m] = factor * (state[m] + force * wides[k])
                        else:
                            state[m] = factor * state[m] + force * wides[k]
            return tuple(state)

        t.store(
            state_ref, lax.fori_loop(0, t.block // ROWS, some, t.load(state_ref))
        )

    return t.call(
        kernel,
        "chunk_state_back" if backward else "chunk_state",
        t.narrow() + t.narrow() + [t.wide_spec(), t.state_spec()],
        t.state_spec(),
        f32(STATE, t.channels),
    )(*[step] * per, *[drive] * per, wide, rate)


def scan_forward(order, step, drive, in_wide, out_wide, rate, entry):
    t = Tiling(order, *step.shape, False)
    per = t.per

    def kernel(_, *refs):
        step_refs, drive_refs = refs[:per], refs[per : 2 * per]
        in_ref, out_ref, rate_ref, entry_ref, y_ref, before_ref, last_ref = refs[2 * per :]

        @pl.when(pl.program_id(1) == 0)
        def _():
            last_ref[...] = entry_ref[...]

        rates = t.load(rate_ref)

        def some(i, state):
            state = list(state)
            base = pl.multiple_of(i * ROWS, ROWS)
            sums = [[None] * ROWS for _ in range(per)]
            for j in range(ROWS):
                token = base + j
                ins, outs = pair(in_ref, token), pair(out_ref, token)
                for g in range(per):
                    now = spread(step_refs[g], token)
                    force = spread(drive_refs[g], token)
                    total = None
                    for k in (0, 1):
                        m = 2 * g + k
                        before_ref[token, 8 * k : 8 * k + 8, t.lanes[g]] = state[m]
                        state[m] = jnp.exp2(now * rates[m]) * state[m] + force * ins[k]
                        term = state[m] * outs[k]
                        total = term if total is None else total + term
                    sums[g][j] = total
            for g in range(per):
                y_ref[pl.ds(base, ROWS), t.lanes[g]] = fold_rows(sums[g])
            return tuple(state)

        t.store(last_ref, lax.fori_loop(0, t.block // ROWS, some, t.load(last_ref)))

    return t.call(
        kernel,
        "scan_forward",
        t.narrow()
        + t.narrow()
        + [t.wide_spec(), t.wide_spec(), t.state_spec(), t.state_spec()],
        (t.token_spec(), t.history_spec(), t.state_spec()),
        (
            f32(t.tokens, t.channels),
            f32(t.tokens, STATE, t.channels),
            f32(STATE, t.channels),
        ),
    )(*[step] * per, *[drive] * per, in_wide, out_wide, rate, entry)


def scan_backward(order, step, drive, back, in_wide, out_wide, rate, entry, before, last):
    t = Tiling(order, *step.shape, True)
    per = t.per

    def kernel(_, *refs):
        step_refs, drive_refs, back_refs = (refs[i * per : (i + 1) * per] for i in range(3))
        in_ref, out_ref, rate_ref, entry_ref, before_ref, last_ref = refs[
            3 * per : 3 * per + 6
        ]
        rate_sum_ref, in_sum_ref, decay_ref, coefficient_ref = refs[3 * per + 6 : 3 * per + 10]
        carry_ref, state_ref, in_part_ref, out_part_ref = refs[3 * per + 10 :]

        @pl.when(pl.program_id(1) == 0)
        def _():
            decay_ref[...] = jnp.zeros_like(decay_ref)
            carry_ref[...] = entry_ref[...]
            state_ref[...] = last_ref[...]

        rates = t.load(rate_ref)

        def some(i, carried):
            carry, state, decay = (list(part) for part in carried)
            base = pl.multiple_of(t.block - ROWS - i * ROWS, ROWS)
            rate_sums = [[None] * ROWS for _ in range(per)]
            in_sums = [[None] * ROWS for _ in range(per)]
            for j in range(ROWS - 1, -1, -1):
                token = base + j
                ins, outs = pair(in_ref, token), pair(out_ref, token)
                in_part, out_part = [None, None], [None, None]
                for g in range(per):
                    now = spread(step_refs[g], token)
                    force = spread(drive_refs[g], token)
                    above = spread(back_refs[g], token)
                    by_rate, by_in = [None, None], [None, None]
                    for k in (0, 1):
                        m = 2 * g + k
                        earlier = before_ref[token, 8 * k : 8 * k + 8, t.lanes[g]]
                        grad = carry[m] + above * outs[k]
                        carry[m] = jnp.exp2(now * rates[m]) * grad
                        weighted = carry[m] * earlier
                        decay[m] = decay[m] + weighted * now
                        by_rate[k] = weighted * rates[m]
                        by_in[k] = grad * ins[k]
                        for parts, term in (
                            (in_part, grad * force),
                            (out_part, above * state[m]),
                        ):
                            parts[k] = term if parts[k] is None else parts[k] + term
                        state[m] = earlier
                    rate_sums[g][j] = by_rate[0] + by_rate[1]
                    in_sums[g][j] = by_in[0] + by_in[1]
                for k in (0, 1):
                    place = pl.multiple_of(token * STATE + k * ROWS, ROWS)
                    in_part_ref[pl.ds(place, ROWS), :] = in_part[k]
                    out_part_ref[pl.ds(place, ROWS), :] = out_part[k]
            for g in range(per):
                rate_sum_ref[pl.ds(base, ROWS), t.lanes[g]] = fold_rows(rate_sums[g])
                in_sum_ref[pl.ds(base, ROWS), t.lanes[g]] = fold_rows(in_sums[g])
            return tuple(carry), tuple(state), tuple(decay)

        carry, state, decay = lax.fori_loop(
            0,
            t.block // ROWS,
            some,
            (t.load(carry_ref), t.load(state_ref), t.load(decay_ref)),
        )
        t.store(carry_ref, carry)
        t.store(state_ref, state)
        t.store(decay_ref, decay)

        for part_ref in (in_part_ref, out_part_ref):
            part = part_ref[...]
            high = low(part)
            ones = jnp.ones((LANES, LANES), jnp.bfloat16)
            part_ref[...] = product(high, ones) + product(
                low(part - high.astype(jnp.float32)), ones
            )
        row = lax.broadcasted_iota(jnp.int32, (ROWS, LANES), 0)
        lane = lax.broadcasted_iota(jnp.int32, (ROWS, LANES), 1)

        def gathered(i, _):
            base = pl.multiple_of(i * ROWS, ROWS)
            tokens = []
            for j in range(ROWS):
                total = None
                for m, part_ref in ((0, in_part_ref), (1, out_part_ref)):
                    for k in (0, 1):
                        place = pl.multiple_of((base + j) * STATE + k * ROWS, ROWS)
                        term = jnp.where(
                            lane == row + (m * STATE + k * ROWS),
                            part_ref[pl.ds(place, ROWS), :],
                            0.0,
                        )
                        total = term if total is None else total + term
                tokens.append(total)
            coefficient_ref[0, pl.ds(base, ROWS), :] = fold_rows(tokens)
            return _

        lax.fori_loop(0, t.block // ROWS, gathered, 0)

    rate_sum, in_sum, decay, coefficients = t.call(
        kernel,
        "scan_backward",
        t.narrow()
        + t.narrow()
        + t.narrow()
        + [
            t.wide_spec(),
            t.wide_spec(),
            t.state_spec(),
            t.state_spec(),
            t.history_spec(),
            t.state_spec(),
        ],
        (t.token_spec(), t.token_spec(), t.state_spec(), t.part_spec()),
        (
            f32(t.tokens, t.channels),
            f32(t.tokens, t.channels),
            f32(STATE, t.channels),
            f32(t.grid[0], t.tokens, LANES),
        ),
        [pltpu.VMEM((STATE, t.width), jnp.float32)] * 2
        + [pltpu.VMEM((t.block * STATE, LANES), jnp.float32)] * 2,
    )(
        *[step] * per,
        *[drive] * per,
        *[back] * per,
        in_wide,
        out_wide,
        rate,
        entry,
        before,
        last,
    )
    return rate_sum, in_sum, decay, jnp.sum(coefficients, 0)[:, : 2 * STATE]


def neighbour_totals(step_total, direction):
    return [
        shift(step_total, "col", direction * distance)
        for distance in range(1, lax.axis_size("col") - 1)
    ]


def chunk_entry(state, totals, rate, direction):
    last = lax.axis_size("col") - 1
    entry = None
    for distance in range(last, 0, -1):
        got = shift(low(state), "col", direction * distance).astype(jnp.float32)
        if entry is not None:
            got = got + jnp.exp2(totals[distance - 1] * rate) * entry
        entry = got
    return entry


def widen(coefficients):
    return jnp.broadcast_to(coefficients[:, :, None], coefficients.shape + (LANES,))


def norm_forward(values, weights):
    inverse = lax.rsqrt(jnp.mean(values * values, axis=1, keepdims=True) + epsilon)
    scaled = values * inverse
    return scaled, inverse, low(scaled * weights)


def norm_backward(upstream, scaled, inverse, weights):
    weighted = upstream * weights
    inner_mean = jnp.mean(weighted * scaled, axis=1, keepdims=True)
    return (
        inverse * (weighted - scaled * inner_mean),
        jnp.sum(upstream * scaled, axis=0, keepdims=True),
    )


def body(
    tokens,
    mixer_norm,
    in_value,
    in_gate,
    conv_weight,
    conv_bias,
    state_proj,
    step_proj,
    step_bias,
    decay_log,
    skip_gain,
    mixer_out,
    feed_norm,
    feed_gate,
    feed_up,
    feed_down,
    out_grad,
):
    channels, units = in_value.shape[1], feed_gate.shape[1]
    order = block_order()
    rows, index = lax.axis_size("row"), lax.axis_index("dp")
    first = gather_weight(jnp.concatenate([in_value, in_gate, mixer_out.T], axis=1))
    in_low, mixer_low = first[:, : 2 * channels], first[:, 2 * channels :]
    feed_low = gather_weight(jnp.concatenate([feed_gate, feed_up], axis=1))
    feed_down_low = gather_weight(feed_down.T)

    inputs = to_whole_features(tokens)
    own_channels = conv_bias.shape[0]
    gains = jnp.stack([mixer_norm, feed_norm]).reshape(-1, own_channels)
    packed = jnp.concatenate(
        [
            gains,
            conv_weight.T,
            conv_bias[None],
            step_bias[None],
            skip_gain[None],
            decay_log.T,
        ],
        axis=0,
    )
    packed = gather_blocks(packed)
    gain_rows = gains.shape[0]
    gains = packed[:, :gain_rows].reshape(-1, 2, mixer_norm.shape[0])
    mixer_gain = gains[:, 0].reshape(1, -1)
    feed_gain = gains[:, 1].reshape(1, -1)
    packed = jnp.swapaxes(packed[:, gain_rows:], 0, 1).reshape(-1, channels)
    taps = packed[:CONV]
    conv_bias_row, step_bias_row, skip_row = (
        packed[CONV + i : CONV + i + 1] for i in range(3)
    )
    decay_rate = -jnp.exp(packed[CONV + 3 :])
    projections = jnp.concatenate([low(step_proj), low(state_proj).T], axis=0)
    projections, inputs = lax.optimization_barrier((projections, inputs))
    half = projections.shape[0] // 2
    projections = gather_blocks(
        lax.dynamic_slice_in_dim(projections, index * half, half, 0)
    )
    projections = both_halves(projections, 1)
    projections = jnp.swapaxes(projections, 0, 1).reshape(-1, channels)
    step_weight, state_low = projections[:DT_RANK], projections[DT_RANK:]
    inputs = inputs.astype(jnp.float32)

    scaled_first, inverse_first, normed_first = norm_forward(inputs, mixer_gain)
    normed_all = row_gather(normed_first)
    count = normed_all.shape[0]
    both_in = product(normed_all, in_low)
    both_in, out_grad = lax.optimization_barrier((both_in, out_grad))
    out_back_low = to_whole_features(out_grad)
    grad_all = row_gather(out_back_low)
    mixer_in, gate_in = both_in[:, :channels], both_in[:, channels:]
    mixer_in = mixer_in.reshape(rows, -1, channels)
    length = mixer_in.shape[1]
    tails = mixer_in[:, -ROWS:]
    outside = shift(block_at(tails, (rows - 1) ^ order), "col", 1)
    earlier = neighbours(outside, tails, order, -1)
    padded = jnp.concatenate([earlier[:, ROWS - CONV + 1 :], mixer_in], axis=1)
    conv_out = conv_bias_row + sum(
        padded[:, k : k + length] * taps[k : k + 1] for k in range(CONV)
    ).reshape(count, channels)
    conv_act = low(sigmoid_linear(conv_out))
    projected = row_total(product(conv_act, state_low, contract_last))
    step_low = low(projected[:, :DT_RANK])
    in_wide = widen(projected[:, DT_RANK : DT_RANK + STATE])
    out_wide = widen(projected[:, DT_RANK + STATE :])
    step_pre = product(step_low, step_weight) + step_bias_row
    step_size = jax.nn.softplus(step_pre)
    act_float = conv_act.astype(jnp.float32)
    drive = step_size * act_float
    rate = decay_rate * LOG2E
    step_total = jnp.sum(step_size, axis=0, keepdims=True)
    earlier_totals = neighbour_totals(step_total, 1)
    later_totals = neighbour_totals(step_total, -1)
    handed = chunk_state(order, step_size, drive, in_wide, rate, False)
    entry = chunk_entry(handed, earlier_totals, rate, 1)
    entry, later_totals = lax.optimization_barrier((entry, later_totals))
    scanned, before, last = scan_forward(
        order, step_size, drive, in_wide, out_wide, rate, entry
    )
    scan_out = scanned + skip_row * act_float
    gate_act = sigmoid_linear(gate_in)
    gated = low(scan_out * gate_act)
    middle = inputs + row_scatter(product(gated, mixer_low, contract_last))

    scaled_second, inverse_second, normed_second = norm_forward(middle, feed_gain)
    normed_feed = row_gather(normed_second)
    both_pre = product(normed_feed, feed_low)
    gate_pre, up_pre = both_pre[:, :units], both_pre[:, units:]
    gate_swish = sigmoid_linear(gate_pre)
    hidden = low(gate_swish * up_pre)
    grad_own, grad_other = feature_halves(grad_all)
    down_grad = add_pair(
        product(grad_own, hidden, contract_first),
        low(product(grad_other, hidden, contract_first)),
    )
    feed_down_low, down_grad = lax.optimization_barrier((feed_down_low, down_grad))
    down_own = scatter_gradient(down_grad)

    hidden_back = product(grad_all, feed_down_low)
    gate_back = low(hidden_back * up_pre * sigmoid_slope(gate_pre))
    up_back = low(hidden_back * gate_swish)
    both_back = jnp.concatenate([gate_back, up_back], axis=1)
    feed_left, feed_right = feature_halves(normed_feed)
    other_grad = low(product(feed_right, both_back, contract_first))
    both_back, other_grad = lax.optimization_barrier((both_back, other_grad))
    normed_back = product(both_back, feed_low, contract_last)
    feed_grad = add_pair(product(feed_left, both_back, contract_first), other_grad)
    normed_back, feed_grad = lax.optimization_barrier((normed_back, feed_grad))
    feed_own = scatter_gradient(feed_grad)
    normed_back = row_scatter(normed_back)
    middle_norm, feed_norm_part = norm_backward(
        normed_back, scaled_second, inverse_second, feed_gain
    )
    middle_back = out_back_low.astype(jnp.float32) + middle_norm
    middle_low, down_own = lax.optimization_barrier((low(middle_back), down_own))
    middle_all = row_gather(middle_low)

    gated_back = product(middle_all, mixer_low)
    scan_back = gated_back * gate_act
    gate_in_back = low(gated_back * scan_out * sigmoid_slope(gate_in))
    normed_own, normed_other = feature_halves(normed_all)
    middle_own, middle_other = feature_halves(middle_all)
    pair_own = jnp.concatenate(
        [
            product(middle_own, gated, contract_first),
            product(normed_own, gate_in_back, contract_first),
        ],
        axis=1,
    )
    pair_other = jnp.concatenate(
        [
            low(product(middle_other, gated, contract_first)),
            low(product(normed_other, gate_in_back, contract_first)),
        ],
        axis=1,
    )
    scan_back, hidden, pair_other = lax.optimization_barrier((scan_back, hidden, pair_other))
    pair_grad = add_pair(pair_own, pair_other)
    output = low(middle + row_scatter(product(hidden, feed_down_low, contract_last)))
    handed_back = chunk_state(order, step_size, scan_back, out_wide, rate, True)
    entry_back = chunk_entry(handed_back, later_totals, rate, -1)
    rate_sum, in_sum, decay_sum, coefficient_back = scan_backward(
        order,
        step_size,
        drive,
        scan_back,
        in_wide,
        out_wide,
        rate,
        entry_back,
        before,
        last,
    )
    rate_sum, in_sum, coefficient_back, pair_grad, output = lax.optimization_barrier(
        (rate_sum, in_sum, coefficient_back, pair_grad, output)
    )
    step_back = rate_sum * LN2 + act_float * in_sum
    act_scan = step_size * in_sum + skip_row * scan_back
    pre_back = step_back * jax.nn.sigmoid(step_pre)
    pre_low = low(pre_back)
    rank_back = product(pre_low, step_weight, contract_last)
    partial = jnp.concatenate([rank_back, coefficient_back], axis=1)
    local, pair_grad, feed_own = lax.optimization_barrier((partial, pair_grad, feed_own))
    proj_back = low(row_total(partial, local))
    pair_own = scatter_gradient(pair_grad)
    act_back = act_scan + product(proj_back, state_low)
    conv_back = act_back * sigmoid_slope(conv_out)
    conv_blocks = conv_back.reshape(rows, length, channels)
    heads = conv_blocks[:, :ROWS]
    outside = shift(block_at(heads, order), "col", -1)
    later = neighbours(outside, heads, order, 1)
    trailing = jnp.concatenate([conv_blocks, later[:, : CONV - 1]], axis=1)
    mixer_back = low(
        sum(
            trailing[:, CONV - 1 - k : CONV - 1 - k + length] * taps[k : k + 1]
            for k in range(CONV)
        )
    ).reshape(count, channels)
    both_in_back = jnp.concatenate([mixer_back, gate_in_back], axis=1)
    normed_first_back = product(both_in_back, in_low, contract_last)
    mixer_back, normed_first_back = lax.optimization_barrier((mixer_back, normed_first_back))
    in_value_grad = add_pair(
        product(normed_own, mixer_back, contract_first),
        low(product(normed_other, mixer_back, contract_first)),
    )
    input_norm, mixer_norm_part = norm_backward(
        row_scatter(normed_first_back), scaled_first, inverse_first, mixer_gain
    )
    tokens_grad = low(middle_back + input_norm)

    def whole(own, after):
        own, _ = lax.optimization_barrier((own, after))
        return both_halves(own, 0)

    feed_grad = whole(feed_own, proj_back)
    down_grad = whole(down_own, proj_back)
    finished = (
        feed_grad[:, :units].astype(jnp.float32),
        feed_grad[:, units:].astype(jnp.float32),
        down_grad.T.astype(jnp.float32),
    )
    gain_parts = jnp.concatenate([mixer_norm_part, feed_norm_part], axis=0)
    in_value_grad, pair_own, tokens_grad, output, gain_parts, *finished = (
        lax.optimization_barrier(
            (in_value_grad, pair_own, tokens_grad, output, gain_parts) + finished
        )
    )
    feed_gate_out, feed_up_out, feed_down_out = finished
    pair_grad = both_halves(pair_own, 0)
    finished = (
        pair_grad[:, channels:].astype(jnp.float32),
        pair_grad[:, :channels].T.astype(jnp.float32),
    )

    def over_tokens(values):
        return jnp.sum(values, axis=0, keepdims=True)

    gain_parts = gain_parts.reshape(2, lax.axis_size("col"), -1, own_channels)
    gain_parts = jnp.swapaxes(gain_parts, 1, 2).reshape(gain_rows, channels)
    packed_grad = jnp.concatenate(
        [gain_parts]
        + [
            jnp.sum(conv_blocks * padded[:, k : k + length], axis=(0, 1))[None]
            for k in range(CONV)
        ]
        + [
            over_tokens(conv_back),
            over_tokens(pre_back),
            over_tokens(scan_back * act_float),
            decay_sum * decay_rate,
        ],
        axis=0,
    )
    projection_grad = jnp.concatenate(
        [
            product(step_low, pre_low, contract_first),
            product(proj_back, conv_act, contract_first),
        ],
        axis=0,
    )
    (output, tokens_grad), (packed_grad, projection_grad, in_value_grad) = to_feature_blocks(
        (output, tokens_grad), (packed_grad, projection_grad, in_value_grad)
    )
    value_own = scatter_gradient(in_value_grad)

    half = projection_grad.shape[0] // 2
    mine, others = (
        lax.dynamic_slice_in_dim(projection_grad, place * half, half, 0)
        for place in (index, 1 - index)
    )
    small = jnp.concatenate(
        [mine + swap(others, "dp", 1), packed_grad + swap(packed_grad, "dp", 1)], axis=0
    )
    small = scatter_by_swaps(small, "col", 1, jnp.bfloat16)
    projection_grad = both_halves(small[:half], 0)
    packed_grad = small[half:]
    gain_sums = packed_grad[:gain_rows]
    distance = 1
    while distance < rows:
        gain_sums = gain_sums + swap(gain_sums, "row", distance)
        distance *= 2
    gain_sums = gain_sums.reshape(2, -1)
    packed_grad = packed_grad[gain_rows:]
    value_own, *finished = lax.optimization_barrier((value_own,) + finished)
    gate_out, mixer_out_grad = finished
    return (
        output,
        tokens_grad.astype(jnp.float32),
        gain_sums[0],
        both_halves(value_own, 0).astype(jnp.float32),
        gate_out,
        packed_grad[:CONV].T,
        packed_grad[CONV],
        projection_grad[DT_RANK:].T,
        projection_grad[:DT_RANK],
        packed_grad[CONV + 1],
        packed_grad[CONV + 3 :].T,
        packed_grad[CONV + 2],
        mixer_out_grad,
        gain_sums[1],
        feed_gate_out,
        feed_up_out,
        feed_down_out,
    )


def solution(mesh):
    token_spec = P(("dp", "row"), "col")
    weight_in, weight_out = P("col", "row"), P("row", "col")
    channel, channel_rows = P(("row", "col")), P(("row", "col"), None)
    parameters = (
        P("col"),
        weight_in,
        weight_in,
        channel_rows,
        channel,
        channel_rows,
        P(None, ("row", "col")),
        channel,
        channel_rows,
        channel,
        weight_out,
        P("col"),
        weight_in,
        weight_in,
        weight_out,
    )
    return jax.shard_map(
        body,
        mesh=mesh,
        in_specs=(token_spec,) + parameters + (token_spec,),
        out_specs=(token_spec, token_spec) + parameters,
        check_vma=False,
    )
```
